32 devices in a mesh: grp: 4 (over y, x), fsdp: 8 (over z, core).
Axes of the slice: x: 2, y: 2, z: 4, core: 2. Of those that a mesh axis runs over, the one named last changes fastest.
Arguments:
- tokens: bfloat16 [32, 1024, 768], P(('grp', 'fsdp')), may hold values from -6 to 6
- segments: int32 [32, 1024], P(('grp', 'fsdp')), may hold values from 0 to 8, as said below
- project_weight: bfloat16 [768, 2304], P('fsdp'), may hold values from -0.21875 to 0.21875
- project_bias: bfloat16 [1536], P('fsdp'), may hold values from -1.796875 to 1.796875
- combine_weight: bfloat16 [768, 768], P('fsdp'), may hold values from -1.75 to 1.75
- combine_bias: bfloat16 [768], P('fsdp'), may hold values from -1.796875 to 1.796875
- first_gain: bfloat16 [768], P('fsdp'), may hold values from 0.5 to 1.5
- first_shift: bfloat16 [768], P('fsdp'), may hold values from -1.796875 to 1.796875
- expand_weight: bfloat16 [768, 3072], P('fsdp'), may hold values from -0.21875 to 0.21875
- expand_bias: bfloat16 [3072], P('fsdp'), may hold values from -1.796875 to 1.796875
- reduce_weight: bfloat16 [3072, 768], P('fsdp'), may hold values from -0.109375 to 0.109375
- reduce_bias: bfloat16 [768], P('fsdp'), may hold values from -1.796875 to 1.796875
- second_gain: bfloat16 [768], P('fsdp'), may hold values from 0.5 to 1.5
- second_shift: bfloat16 [768], P('fsdp'), may hold values from -1.796875 to 1.796875
- layer_cotangent: bfloat16 [32, 1024, 768], P(('grp', 'fsdp')), may hold values from -6 to 6
- pooled_cotangent: float32 [32, 8, 768], P(('grp', 'fsdp')), may hold values from -192 to 192
Outputs:
- layer_output: bfloat16 [32, 1024, 768], P(('grp', 'fsdp'))
- pooled: float32 [32, 8, 768], P(('grp', 'fsdp'))
- token_gradient: bfloat16 [32, 1024, 768], P(('grp', 'fsdp'))
- project_weight_grad: float32 [768, 2304], P('fsdp')
- project_bias_grad: float32 [1536], P('fsdp')
- combine_weight_grad: float32 [768, 768], P('fsdp')
- combine_bias_grad: float32 [768], P('fsdp')
- first_gain_grad: float32 [768], P('fsdp')
- first_shift_grad: float32 [768], P('fsdp')
- expand_weight_grad: float32 [768, 3072], P('fsdp')
- expand_bias_grad: float32 [3072], P('fsdp')
- reduce_weight_grad: float32 [3072, 768], P('fsdp')
- reduce_bias_grad: float32 [768], P('fsdp')
- second_gain_grad: float32 [768], P('fsdp')
- second_shift_grad: float32 [768], P('fsdp')
The draws below stay inside these ranges and needn't reach their ends.
Inputs may be any that keep to these rules, and one draw needn't show every extreme that they name: `segments`: in every row the nonzero ids start at 1 at the row's first token and run 1, 2, 3 and so on, each crop one contiguous run of tokens; padding tokens (0) come only after the last crop of a row.
All inputs are finite; a program needn't handle non-finite values.
Results may differ from the reference program's by a relative error of at most 0.013.
Values may be sent and summed in bfloat16 or wider, within the bound.
No kernel may reach another device: no remote copies, remote signals or barrier semaphores. Data moves between devices by JAX's collectives and lax.ppermute only.
A program may use at most 320 MiB of HBM per device.

```python
from functools import partial
import jax
import jax.numpy as jnp
from jax import lax

D = 768
H = 12
DH = 64
FF = 3072
L = 1024
SEG = 8
ROWS = 32


def draw_segments(key, part):
    lengths = jax.random.randint(key, (ROWS, SEG), L // 64, L // 4 + 1, dtype=jnp.int32)
    crop_ends = jnp.cumsum(lengths, axis=1)
    position = jnp.arange(L, dtype=jnp.int32)
    passed = jnp.sum((crop_ends[:, None, :] <= position[None, :, None]).astype(jnp.int32), axis=2)
    return jnp.where(passed < SEG, passed + 1, 0).astype(jnp.int32)


def block_levels(rng, shape, cuts, least, high):
    def one(dim, shards_of):
        heights = jax.random.uniform(jax.random.fold_in(jax.random.fold_in(rng, 6), dim), (shards_of,), jnp.float32, least / len(cuts), high / len(cuts))
        return jnp.repeat(jnp.exp(heights), shape[dim] // shards_of).reshape((-1,) + (1,) * (len(shape) - dim - 1))

    level = one(*cuts[0])
    for cut in cuts[1:]:
        level = level * one(*cut)
    return level


def gaussian(own_key, dims, scale, limit, split=(), kind=jnp.bfloat16):
    factor_of = block_levels(own_key, dims, split, -0.22, 0.18) if split else 1.0
    array = jax.random.normal(own_key, dims, jnp.float32) * scale * factor_of
    return jnp.minimum(jnp.maximum(array, -limit), limit).astype(kind)


def setup_inputs(seed: int = 0) -> dict:
    seeds = jax.random.split(jax.random.key(seed), 17)
    tokens = gaussian(seeds[0], (ROWS, L, D), 1.0, 6.0, ((0, 32),))
    segments = draw_segments(jax.random.fold_in(seeds[16], 71), 0)
    project_weight = gaussian(seeds[2], (D, 3 * D), D ** -0.5, 0.21875, ((0, 8),))
    project_bias = gaussian(seeds[3], (2 * D,), 0.3, 1.796875, ((0, 8),))
    combine_weight = gaussian(seeds[4], (D, D), (D // 64) ** -0.5, 1.75, ((0, 8),))
    combine_bias = gaussian(seeds[5], (D,), 0.3, 1.796875, ((0, 8),))
    first_gain = jnp.clip(1.0 + 0.1 * jax.random.normal(seeds[6], (D,), jnp.float32), 0.5, 1.5).astype(jnp.bfloat16)
    first_shift = gaussian(seeds[7], (D,), 0.3, 1.796875, ((0, 8),))
    expand_weight = gaussian(seeds[8], (D, FF), D ** -0.5, 0.21875, ((0, 8),))
    expand_bias = gaussian(seeds[9], (FF,), 0.3, 1.796875, ((0, 8),))
    reduce_weight = gaussian(seeds[10], (FF, D), FF ** -0.5, 0.109375, ((0, 8),))
    reduce_bias = gaussian(seeds[11], (D,), 0.3, 1.796875, ((0, 8),))
    second_gain = jnp.clip(1.0 + 0.1 * jax.random.normal(seeds[12], (D,), jnp.float32), 0.5, 1.5).astype(jnp.bfloat16)
    second_shift = gaussian(seeds[13], (D,), 0.3, 1.796875, ((0, 8),))
    layer_cotangent = gaussian(seeds[14], (ROWS, L, D), 1.0, 6.0, ((0, 32),))
    pooled_cotangent = gaussian(seeds[15], (ROWS, SEG, D), 32.0, 192.0, ((0, 32),), jnp.float32)
    return {"tokens": tokens, "segments": segments, "project_weight": project_weight, "project_bias": project_bias, "combine_weight": combine_weight, "combine_bias": combine_bias, "first_gain": first_gain, "first_shift": first_shift, "expand_weight": expand_weight, "expand_bias": expand_bias, "reduce_weight": reduce_weight, "reduce_bias": reduce_bias, "second_gain": second_gain, "second_shift": second_shift, "layer_cotangent": layer_cotangent, "pooled_cotangent": pooled_cotangent}


NEG_FILL = -1e+30
EPSILON = 1e-12

@jax.custom_vjp
def low(v):
    return lax.optimization_barrier(v.astype(jnp.bfloat16)).astype(jnp.float32)

@jax.custom_vjp
def low_back(v):
    return v

def low_keep(v):
    return (low(v), None)

def low_pass(kept, grad):
    return (grad,)

def back_keep(v):
    return (v, None)

def back_low(kept, grad):
    return (low(grad),)
low.defvjp(low_keep, low_pass)
low_back.defvjp(back_keep, back_low)

def product(left, right):
    return jnp.dot(left, right, precision=lax.Precision.HIGHEST, preferred_element_type=jnp.float32)

def layer_norm(values, norm_gain, norm_shift):
    average = lax.optimization_barrier(jnp.mean(values, axis=-1, keepdims=True))
    centred = values - average
    variance = lax.optimization_barrier(jnp.mean(centred * centred, axis=-1, keepdims=True))
    return centred * lax.rsqrt(variance + EPSILON) * norm_gain + norm_shift

def attend_group(packed):
    query_grp, keys_grp, values_grp, seg_grp = packed
    scores = jnp.einsum('gqhd,gkhd->ghqk', query_grp, keys_grp, precision=lax.Precision.HIGHEST) * DH ** (-0.5)
    scores = low_back(scores)
    allowed = (seg_grp[:, :, None] == seg_grp[:, None, :])[:, None]
    masked = jnp.where(allowed, scores, NEG_FILL)
    highest = lax.optimization_barrier(jnp.max(masked, axis=-1, keepdims=True))
    exponent = jnp.exp(masked - highest)
    weights_low = low(exponent / lax.optimization_barrier(jnp.sum(exponent, axis=-1, keepdims=True)))
    return jnp.einsum('ghqk,gkhd->gqhd', weights_low, values_grp, precision=lax.Precision.HIGHEST)

def forward(segments, tokens, project_weight, project_bias, combine_weight, combine_bias, first_gain, first_shift, expand_weight, expand_bias, reduce_weight, reduce_bias, second_gain, second_shift):
    rows_all = segments.shape[0]
    flat = tokens.reshape(-1, D)
    bias_all = jnp.concatenate([project_bias[:D], jnp.zeros((D,), project_bias.dtype), project_bias[D:]])
    triple = low(low_back(product(flat, project_weight) + bias_all))
    shaped = triple.reshape(rows_all // 2, 2, L, 3, H, DH)
    grouped = segments.reshape(rows_all // 2, 2, L)
    context = lax.map(jax.checkpoint(attend_group), (shaped[:, :, :, 0], shaped[:, :, :, 1], shaped[:, :, :, 2], grouped))
    context = low(low_back(context.reshape(-1, D)))
    attn_out = low_back(product(context, combine_weight) + combine_bias)
    hidden = layer_norm(flat + attn_out, first_gain, first_shift)
    pre_act = low_back(product(low(hidden), expand_weight) + expand_bias)
    activ = low(jax.nn.gelu(pre_act, approximate=False))
    branch = low_back(product(activ, reduce_weight) + reduce_bias)
    result = layer_norm(hidden + branch, second_gain, second_shift)
    result_rows = result.reshape(rows_all, L, D)
    slot_ids = jnp.arange(1, SEG + 1, dtype=jnp.int32)
    member = (segments[:, None, :] == slot_ids[None, :, None]).astype(result.dtype)
    divisor = jnp.maximum(lax.optimization_barrier(jnp.sum(member, axis=2)), 1.0)[..., None]
    pooled = jnp.einsum('rsl,rld->rsd', member, result_rows, precision=lax.Precision.HIGHEST) / divisor
    return (result_rows, pooled)

def reference(tokens, segments, project_weight, project_bias, combine_weight, combine_bias, first_gain, first_shift, expand_weight, expand_bias, reduce_weight, reduce_bias, second_gain, second_shift, layer_cotangent, pooled_cotangent):
    params = (project_weight, project_bias, combine_weight, combine_bias, first_gain, first_shift, expand_weight, expand_bias, reduce_weight, reduce_bias, second_gain, second_shift)
    widened = tuple((entry.astype(jnp.float32) for entry in params))
    outputs, pullback = jax.vjp(partial(forward, segments), tokens.astype(jnp.float32), *widened)
    result_rows, pooled = outputs
    grads = pullback((layer_cotangent.astype(jnp.float32), pooled_cotangent.astype(jnp.float32)))
    factor = (ROWS * L) ** (-0.5)
    scaled = tuple((entry * factor for entry in grads[1:]))
    return (result_rows.astype(jnp.bfloat16), pooled, grads[0].astype(jnp.bfloat16), scaled[0], scaled[1], scaled[2], scaled[3], scaled[4], scaled[5], scaled[6], scaled[7], scaled[8], scaled[9], scaled[10], scaled[11])
```

```python
from functools import partial

import jax
import jax.numpy as jnp
from jax import lax
from jax.experimental import pallas as pl
from jax.experimental.pallas import tpu as pltpu
from jax.sharding import PartitionSpec as P

H = 12
DH = 64
SEG = 8
LANES = 128
NEG_FILL = -1e30
EPSILON = 1e-12
BF16 = jnp.bfloat16
F32 = jnp.float32

TAIL_P = 0.33
TAIL = (
    0.13275454438237264,
    0.11835055488372218,
    0.18469205342974412,
    -0.0957394408156175,
    0.3375615034491361,
    -0.2238704213061762,
    0.04625121306008233,
)
LOG2E = 1.4426950408889634
INV_SQRT_2PI = 0.3989422804014327


def cost(flops, *arrays):
    moved = sum(a.size * a.dtype.itemsize for a in arrays)
    return pl.CostEstimate(flops=int(flops), transcendentals=0, bytes_accessed=int(moved))


def nn(left, right):
    return lax.dot_general(left, right, (((1,), (0,)), ((), ())), preferred_element_type=F32)


def nt(left, right):
    return lax.dot_general(left, right, (((1,), (1,)), ((), ())), preferred_element_type=F32)


def tn(left, right):
    return lax.dot_general(left, right, (((0,), (0,)), ((), ())), preferred_element_type=F32)


def shape_of(dims, kind):
    return jax.ShapeDtypeStruct(dims, kind)


def full_spec(dims):
    return pl.BlockSpec(dims, lambda *_: (0,) * len(dims))


def normal_parts(x):
    bell = jnp.exp2(x * x * (-0.5 * LOG2E))
    t = 1.0 / (1.0 + TAIL_P * jnp.abs(x))
    poly = jnp.full_like(t, TAIL[-1])
    for coefficient in TAIL[-2::-1]:
        poly = poly * t + coefficient
    tail = poly * t * bell
    return jnp.where(x >= 0, 1.0 - tail, tail), bell * INV_SQRT_2PI


def project_kernel(x_ref, w_ref, b_ref, o_ref):
    rows = x_ref.shape[0]
    step = min(256, rows)
    for at in range(0, rows, step):
        o_ref[0, at : at + step, :] = (nn(x_ref[at : at + step, :], w_ref[0]) + b_ref[0]).astype(BF16)


def project(x, weights, bias):
    rows, width = x.shape
    half = width // 2
    return pl.pallas_call(
        project_kernel,
        out_shape=shape_of((3, rows, width), BF16),
        grid=(3, 2),
        in_specs=[
            full_spec((rows, width)),
            pl.BlockSpec((1, width, half), lambda t, j: (t, 0, j)),
            pl.BlockSpec((1, 1, half), lambda t, j: (t, 0, j)),
        ],
        out_specs=pl.BlockSpec((1, rows, half), lambda t, j: (t, 0, j)),
        cost_estimate=cost(6 * rows * width * width, x, weights),
        name="project",
    )(x, weights, bias)


def window_sizes(block, length):
    sizes = [block + extra for extra in (128, 256, 384, 512) if block + extra < length]
    return sizes + [length]


def key_limits(seg, block):
    length = seg.shape[0]
    rows = seg.reshape(length // block, block)
    place = jnp.arange(length, dtype=jnp.int32)[None, :]
    low = jnp.min(jnp.where(seg[None, :] == rows[:, :1], place, length), axis=1)
    high = jnp.max(jnp.where(seg[None, :] == rows[:, -1:], place + 1, 0), axis=1)
    low = low // LANES * LANES
    sizes = window_sizes(block, length)
    size = jnp.full_like(low, sizes[-1])
    for candidate in sizes[-2::-1]:
        size = jnp.where(high - low <= candidate, candidate, size)
    return jnp.stack([jnp.minimum(low, length - size), size])


def for_window(limits_ref, block, sizes, body):
    start = limits_ref[0, block]
    for size in sizes:

        @pl.when(limits_ref[1, block] == size)
        def _(size=size):
            body(pl.multiple_of(start, LANES), size)


def attend_forward_kernel(sizes, limits_ref, q_ref, k_ref, v_ref, segq_ref, segk_ref, o_ref, lse_ref):
    first = lax.broadcasted_iota(jnp.int32, (1, LANES), 1) < DH
    rows = q_ref.shape[1]
    scale = jnp.asarray(DH ** (-0.5), BF16)

    def body(start, size):
        query = q_ref[0] * scale
        keys = k_ref[0, pl.ds(start, size), :]
        values = v_ref[0, pl.ds(start, size), :]
        allowed = segq_ref[...] == segk_ref[:, pl.ds(start, size)]
        parts = []
        stats = []
        for mine in (first, jnp.logical_not(first)):
            scores = nt(jnp.where(mine, query, jnp.zeros_like(query)), keys)
            scores = jnp.where(allowed, scores, NEG_FILL)
            highest = jnp.max(scores, axis=1, keepdims=True)
            exponent = jnp.exp(scores - highest)
            total = jnp.sum(exponent, axis=1, keepdims=True)
            parts.append(nn(exponent.astype(BF16), values) / total)
            stats.append(highest + jnp.log(total))
        o_ref[...] = jnp.where(first, parts[0], parts[1]).astype(BF16)
        both = jnp.where(first, stats[0], stats[1])
        flipped = both.T
        lse_ref[0, 0:1, :] = flipped[0:1, :]
        lse_ref[0, 1:2, :] = flipped[DH : DH + 1, :]

    for_window(limits_ref, pl.program_id(1), sizes, body)


def attend_forward(qkv, limits, seg_column, seg_row, block):
    _, length, width = qkv.shape
    pairs = width // LANES
    return pl.pallas_call(
        partial(attend_forward_kernel, window_sizes(block, length)),
        out_shape=(shape_of((length, width), BF16), shape_of((pairs, 8, length), F32)),
        grid_spec=pltpu.PrefetchScalarGridSpec(
            num_scalar_prefetch=1,
            grid=(pairs, length // block),
            in_specs=[
                pl.BlockSpec((1, block, LANES), lambda p, b, _: (0, b, p)),
                pl.BlockSpec((1, length, LANES), lambda p, b, _: (1, 0, p)),
                pl.BlockSpec((1, length, LANES), lambda p, b, _: (2, 0, p)),
                pl.BlockSpec((block, 1), lambda p, b, _: (b, 0)),
                pl.BlockSpec((1, length), lambda p, b, _: (0, 0)),
            ],
            out_specs=[
                pl.BlockSpec((block, LANES), lambda p, b, _: (b, p)),
                pl.BlockSpec((1, 8, block), lambda p, b, _: (p, 0, b)),
            ],
        ),
        cost_estimate=cost(8 * length * length * width, qkv),
        name="attend_forward",
    )(limits, qkv, qkv, qkv, seg_column, seg_row)


def attend_backward_kernel(
    sizes,
    limits_ref,
    q_ref,
    k_ref,
    v_ref,
    d_ref,
    lse_ref,
    segk_ref,
    segq_ref,
    grad_ref,
    sums_ref,
    dk_ref,
    dv_ref,
    dq_ref,
):
    block = pl.program_id(1)
    first = lax.broadcasted_iota(jnp.int32, (1, LANES), 1) < DH
    rows = q_ref.shape[1]
    scale = jnp.asarray(DH ** (-0.5), BF16)

    @pl.when(block == 0)
    def _():
        dk_ref[...] = jnp.zeros_like(dk_ref)
        dv_ref[...] = jnp.zeros_like(dv_ref)

    def body(start, size):
        query = q_ref[0] * scale
        grads = d_ref[...]
        keys = k_ref[0, pl.ds(start, size), :]
        values = v_ref[0, pl.ds(start, size), :]
        allowed = segk_ref[pl.ds(start, size), :] == segq_ref[...]
        grad_query = []
        grad_key = None
        for h, mine in enumerate((first, jnp.logical_not(first))):
            query_h = jnp.where(mine, query, jnp.zeros_like(query))
            grads_h = jnp.where(mine, grads, jnp.zeros_like(grads))
            scores = nt(keys, query_h)
            weights = jnp.where(allowed, jnp.exp(scores - lse_ref[0, h : h + 1, :]), 0.0)
            grad_weights = nt(values, grads_h)
            inner = jnp.sum(weights * grad_weights, axis=0, keepdims=True)
            grad_scores = (weights * (grad_weights - inner)).astype(BF16)
            dv_h = nn(weights.astype(BF16), grads_h)
            dk_h = nn(grad_scores, query_h)
            grad_query.append(tn(grad_scores, keys))
            grad_key, grad_value = (dk_h, dv_h) if grad_key is None else (grad_key + dk_h, grad_value + dv_h)
        dk_ref[pl.ds(start, size), :] += grad_key
        dv_ref[pl.ds(start, size), :] += grad_value
        place = pl.ds(pl.multiple_of(block * rows, rows), rows)
        dq_ref[place, :] = jnp.where(first, grad_query[0], grad_query[1]) * (DH ** (-0.5))

    for_window(limits_ref, block, sizes, body)

    @pl.when(block == pl.num_programs(1) - 1)
    def _():
        for t, source in enumerate((dq_ref, dk_ref, dv_ref)):
            low = source[...].astype(BF16)
            grad_ref[t] = low
            if t != 1:
                sums_ref[t : t + 1, :] = jnp.sum(low.astype(F32), axis=0, keepdims=True)


def attend_backward(qkv, grad_context, lse, limits, seg_column, seg_row, block, base, pairs, earlier=None):
    _, length, width = qkv.shape
    anywhere = pl.BlockSpec(memory_space=pl.ANY)
    made = (shape_of((3, length, width), BF16), shape_of((8, width), F32))
    kernel = partial(attend_backward_kernel, window_sizes(block, length))
    if earlier is not None:
        inner = kernel

        def kernel(limits_ref, *refs):
            inner(limits_ref, *refs[:7], *refs[9:])

    return pl.pallas_call(
        kernel,
        out_shape=made,
        grid_spec=pltpu.PrefetchScalarGridSpec(
            num_scalar_prefetch=1,
            grid=(pairs, length // block),
            in_specs=[
                pl.BlockSpec((1, block, LANES), lambda p, b, _: (0, b, base + p)),
                pl.BlockSpec((1, length, LANES), lambda p, b, _: (1, 0, base + p)),
                pl.BlockSpec((1, length, LANES), lambda p, b, _: (2, 0, base + p)),
                pl.BlockSpec((block, LANES), lambda p, b, _: (b, base + p)),
                pl.BlockSpec((1, 8, block), lambda p, b, _: (base + p, 0, b)),
                pl.BlockSpec((length, 1), lambda p, b, _: (0, 0)),
                pl.BlockSpec((1, block), lambda p, b, _: (0, b)),
            ]
            + ([] if earlier is None else [anywhere] * 2),
            out_specs=[
                pl.BlockSpec((3, length, LANES), lambda p, b, _: (0, 0, base + p)),
                pl.BlockSpec((8, LANES), lambda p, b, _: (0, base + p)),
            ],
            scratch_shapes=[pltpu.VMEM((length, LANES), F32)] * 3,
        ),
        input_output_aliases={} if earlier is None else {8: 0, 9: 1},
        cost_estimate=cost(12 * length * length * LANES * pairs, qkv),
        name="attend_backward",
    )(limits, qkv, qkv, qkv, grad_context, lse, seg_column, seg_row, *(earlier or ()))


def norm_values(values, gain, shift):
    average = jnp.mean(values, axis=-1, keepdims=True)
    centred = values - average
    variance = jnp.mean(centred * centred, axis=-1, keepdims=True)
    inverse = lax.rsqrt(variance + EPSILON)
    normed = centred * inverse
    return normed * gain + shift, normed, inverse


def norm_pull(grad_out, normed, inverse, gain):
    scaled = grad_out * gain
    mean_scaled = jnp.mean(scaled, axis=-1, keepdims=True)
    mean_product = jnp.mean(scaled * normed, axis=-1, keepdims=True)
    return inverse * (scaled - mean_scaled - normed * mean_product)


def column_sum(values):
    return jnp.sum(values, axis=0, keepdims=True)


def combine_kernel(c_ref, w_ref, x_ref, vec_ref, hidden_ref, low_ref, normed_ref, inverse_ref):
    attn = nn(c_ref[...], w_ref[0]) + vec_ref[0:1, :]
    hidden, normed, inverse = norm_values(x_ref[...].astype(F32) + attn, vec_ref[1:2, :], vec_ref[2:3, :])
    hidden_ref[...] = hidden
    low_ref[...] = hidden.astype(BF16)
    normed_ref[...] = normed
    inverse_ref[...] = inverse


def combine(context, weights, tokens, vectors, block):
    rows, width = context.shape
    row_spec = pl.BlockSpec((block, width), lambda b: (b, 0))
    return pl.pallas_call(
        combine_kernel,
        out_shape=(
            shape_of((rows, width), F32),
            shape_of((rows, width), BF16),
            shape_of((rows, width), F32),
            shape_of((rows, 1), F32),
        ),
        grid=(rows // block,),
        in_specs=[
            row_spec,
            pl.BlockSpec((1, width, width), lambda b: (3, 0, 0)),
            row_spec,
            full_spec(vectors.shape),
        ],
        out_specs=[row_spec, row_spec, row_spec, pl.BlockSpec((block, 1), lambda b: (b, 0))],
        cost_estimate=cost(4 * rows * width * width, context, tokens),
        name="combine",
    )(context, weights, tokens, vectors)


def expand_kernel(x_ref, w_ref, b_ref, act_ref, slope_ref):
    rows = x_ref.shape[0]
    step = min(256, rows)
    for at in range(0, rows, step):
        pre = nn(x_ref[at : at + step, :], w_ref[0]) + b_ref[0]
        mass, bell = normal_parts(pre)
        act_ref[at : at + step, :] = (pre * mass).astype(BF16)
        slope_ref[at : at + step, :] = (mass + pre * bell).astype(BF16)


def expand(hidden_low, weights, bias):
    rows, width = hidden_low.shape
    count = weights.shape[0]
    half = width // 2
    out_spec = pl.BlockSpec((rows, half), lambda t, j: (0, 2 * t + j))
    return pl.pallas_call(
        expand_kernel,
        out_shape=(shape_of((rows, count * width), BF16),) * 2,
        grid=(count, 2),
        in_specs=[
            full_spec((rows, width)),
            pl.BlockSpec((1, width, half), lambda t, j: (t, 0, j)),
            pl.BlockSpec((1, 1, half), lambda t, j: (t, 0, j)),
        ],
        out_specs=[out_spec, out_spec],
        cost_estimate=cost(12 * rows * count * width * width // 3, hidden_low, weights),
        name="expand",
    )(hidden_low, weights, bias)


def reduce_kernel(
    act_ref,
    w_ref,
    hidden_ref,
    vec_ref,
    cot_ref,
    pooled_cot_ref,
    seg_col_ref,
    seg_row_ref,
    out_ref,
    pooled_ref,
    grad_ref,
    grad_low_ref,
    sums_ref,
    share_ref,
):
    at = pl.program_id(0)
    rows = act_ref.shape[0]
    slot = lax.broadcasted_iota(jnp.int32, (16, 1), 0) + 1
    counts = jnp.sum((seg_row_ref[...] == slot).astype(F32), axis=1, keepdims=True)
    divisor = jnp.maximum(counts, 1.0)

    @pl.when(at == 0)
    def _():
        share_ref[...] = jnp.zeros_like(share_ref)
        share = pooled_cot_ref[...] / divisor[0:SEG]
        high = share.astype(BF16).astype(F32)
        share_ref[0:SEG, :] = high
        share_ref[2 * SEG : 3 * SEG, :] = share - high
        sums_ref[...] = jnp.zeros_like(sums_ref)
        pooled_ref[...] = jnp.zeros_like(pooled_ref)

    gain = vec_ref[1:2, :]
    branch = nn(act_ref[...], w_ref[...]) + vec_ref[0:1, :]
    result, normed, inverse = norm_values(hidden_ref[...] + branch, gain, vec_ref[2:3, :])
    out_ref[...] = result.astype(BF16)
    place = pl.ds(pl.multiple_of(at * rows, rows), rows)
    member = (seg_row_ref[:, place] == slot).astype(BF16)
    high = result.astype(BF16)
    rest = (result - high.astype(F32)).astype(BF16)
    pooled_ref[...] += (nn(member, high) + nn(member, rest))[0:SEG]
    lane = lax.broadcasted_iota(jnp.int32, (1, LANES), 1)
    chosen = jnp.where(lane < 2 * SEG, lane + 1, lane - 2 * SEG + 1)
    chosen = jnp.where(lane % (2 * SEG) < SEG, chosen, -1)
    chosen = jnp.where(lane < 4 * SEG, chosen, -1)
    spread = nn((seg_col_ref[...] == chosen).astype(BF16), share_ref[...].astype(BF16))
    grad_result = cot_ref[...].astype(F32) + spread
    grad_second = norm_pull(grad_result, normed, inverse, gain)
    grad_low = grad_second.astype(BF16)
    grad_ref[...] = grad_second
    grad_low_ref[...] = grad_low
    sums_ref[0:1, :] += column_sum(grad_result * normed)
    sums_ref[1:2, :] += column_sum(grad_result)
    sums_ref[2:3, :] += column_sum(grad_low.astype(F32))

    @pl.when(at == pl.num_programs(0) - 1)
    def _():
        pooled_ref[...] = pooled_ref[...] / divisor[0:SEG]


def reduce(act, weights, hidden, vectors, cotangent, pooled_cotangent, seg_column, seg_row, block):
    rows, width = hidden.shape
    depth = act.shape[1]
    row_spec = pl.BlockSpec((block, width), lambda b: (b, 0))
    return pl.pallas_call(
        reduce_kernel,
        out_shape=(
            shape_of((rows, width), BF16),
            shape_of((SEG, width), F32),
            shape_of((rows, width), F32),
            shape_of((rows, width), BF16),
            shape_of((8, width), F32),
        ),
        grid=(rows // block,),
        in_specs=[
            pl.BlockSpec((block, depth), lambda b: (b, 0)),
            full_spec(weights.shape),
            row_spec,
            full_spec(vectors.shape),
            row_spec,
            full_spec(pooled_cotangent.shape),
            pl.BlockSpec((block, 1), lambda b: (b, 0)),
            full_spec(seg_row.shape),
        ],
        out_specs=[
            row_spec,
            full_spec((SEG, width)),
            row_spec,
            row_spec,
            full_spec((8, width)),
        ],
        scratch_shapes=[pltpu.VMEM((LANES, width), F32)],
        cost_estimate=cost(3 * rows * width * depth, act, weights),
        name="reduce",
    )(act, weights, hidden, vectors, cotangent, pooled_cotangent, seg_column, seg_row)


def grad_pre_kernel(g_ref, w_ref, slope_ref, o_ref, sums_ref):
    rows = g_ref.shape[0]
    step = min(256, rows)
    total = None
    for at in range(0, rows, step):
        grad = nt(g_ref[at : at + step, :], w_ref[...]) * slope_ref[at : at + step, :].astype(F32)
        low = grad.astype(BF16)
        o_ref[at : at + step, :] = low
        part = column_sum(low.astype(F32))
        total = part if total is None else total + part
    sums_ref[...] = jnp.broadcast_to(total, sums_ref.shape)


def grad_pre_of(grad_branch, weights, slope):
    rows, width = grad_branch.shape
    depth = weights.shape[0]
    half = width // 2
    return pl.pallas_call(
        grad_pre_kernel,
        out_shape=(shape_of((rows, depth), BF16), shape_of((8, depth), F32)),
        grid=(depth // half,),
        in_specs=[
            full_spec((rows, width)),
            pl.BlockSpec((half, width), lambda j: (j, 0)),
            pl.BlockSpec((rows, half), lambda j: (0, j)),
        ],
        out_specs=[
            pl.BlockSpec((rows, half), lambda j: (0, j)),
            pl.BlockSpec((8, half), lambda j: (0, j)),
        ],
        cost_estimate=cost(3 * rows * width * depth, grad_branch, weights),
        name="grad_pre",
    )(grad_branch, weights, slope)


def grad_hidden_kernel(
    gp_ref, we_ref, second_ref, normed_ref, inverse_ref, vec_ref, wc_ref, first_ref, low_ref, context_ref, sums_ref
):
    @pl.when(pl.program_id(0) == 0)
    def _():
        sums_ref[...] = jnp.zeros_like(sums_ref)

    width = second_ref.shape[1]
    grad_hidden = second_ref[...]
    for t in range(we_ref.shape[0]):
        grad_hidden += nt(gp_ref[:, t * width : (t + 1) * width], we_ref[t])
    normed = normed_ref[...]
    grad_first = norm_pull(grad_hidden, normed, inverse_ref[...], vec_ref[1:2, :])
    low = grad_first.astype(BF16)
    first_ref[...] = grad_first
    low_ref[...] = low
    context_ref[...] = nt(low, wc_ref[0]).astype(BF16)
    sums_ref[0:1, :] += column_sum(grad_hidden * normed)
    sums_ref[1:2, :] += column_sum(grad_hidden)
    sums_ref[2:3, :] += column_sum(low.astype(F32))


def grad_hidden_of(grad_pre, expand_weights, grad_second, normed, inverse, vectors, attend_weights, block):
    rows, width = grad_second.shape
    row_spec = pl.BlockSpec((block, width), lambda b: (b, 0))
    return pl.pallas_call(
        grad_hidden_kernel,
        out_shape=(
            shape_of((rows, width), F32),
            shape_of((rows, width), BF16),
            shape_of((rows, width), BF16),
            shape_of((8, width), F32),
        ),
        grid=(rows // block,),
        in_specs=[
            pl.BlockSpec((block, grad_pre.shape[1]), lambda b: (b, 0)),
            full_spec(expand_weights.shape),
            row_spec,
            row_spec,
            pl.BlockSpec((block, 1), lambda b: (b, 0)),
            full_spec(vectors.shape),
            pl.BlockSpec((1, width, width), lambda b: (3, 0, 0)),
        ],
        out_specs=[row_spec, row_spec, row_spec, full_spec((8, width))],
        cost_estimate=cost(12 * rows * width * width, grad_pre, expand_weights),
        name="grad_hidden",
    )(grad_pre, expand_weights, grad_second, normed, inverse, vectors, attend_weights)


def token_grad_kernel(g_ref, w_ref, first_ref, o_ref):
    total = first_ref[...]
    for t in range(3):
        total += nt(g_ref[t], w_ref[t])
    o_ref[...] = total.astype(BF16)


def token_grad_of(grad_qkv, weights, grad_first, block):
    rows, width = grad_first.shape
    row_spec = pl.BlockSpec((block, width), lambda b: (b, 0))
    return pl.pallas_call(
        token_grad_kernel,
        out_shape=shape_of((rows, width), BF16),
        grid=(rows // block,),
        in_specs=[
            pl.BlockSpec((3, block, width), lambda b: (0, b, 0)),
            pl.BlockSpec((3, width, width), lambda b: (0, 0, 0)),
            row_spec,
        ],
        out_specs=row_spec,
        cost_estimate=cost(6 * rows * width * width, grad_qkv, weights),
        name="token_grad",
    )(grad_qkv, weights, grad_first)


AXES = ("grp", "fsdp")
TAIL_ROWS = 8


def hop(value, shards, move):
    pairs = []
    for g in range(4):
        for f in range(shards):
            to_g, to_f = move(g, f)
            pairs.append((g * shards + f, to_g * shards + to_f))
    return lax.ppermute(value, AXES, pairs)


def along(value, shards, by):
    return hop(value, shards, lambda g, f: (g, (f + 2 * by) % shards))


def swap_first(value, shards):
    return hop(value, shards, lambda g, f: (g ^ (1 + f % 2), f))


def swap_second(value, shards):
    return hop(value, shards, lambda g, f: (g ^ (2 - f % 2), f))


def swap_core(value, shards):
    return hop(value, shards, lambda g, f: (g, f ^ 1))


def after(value, *others):
    return lax.optimization_barrier((value, *others))[0]


def chain_of(block, shards):
    return jnp.stack([block] + [along(block, shards, by) for by in range(1, shards // 2)])


def near_of(chain, shards):
    return jnp.concatenate([chain, swap_first(chain, shards)])


def assemble_kernel(shard, depth, by_rows, has_tail, me_ref, *refs):
    sources, (out_ref, *tail), sems = refs[:4], refs[4:-1], refs[-1]
    g0, z0, c0 = me_ref[0], me_ref[1], me_ref[2]
    copies = []

    def copy(source, target):
        made = pltpu.make_async_copy(source, target, sems.at[len(copies)])
        made.start()
        copies.append(made)

    for k, source in enumerate(sources):
        core = c0 if k < 2 else 1 - c0
        for t in range(2):
            part = g0 ^ (t * (1 + core)) ^ ((k % 2) * (2 - core))
            for s in range(depth):
                place = lax.rem(z0 + depth - s, depth) * 2 + core
                at = t * depth + s
                block = source.at[at, pl.ds(0, shard), :]
                if by_rows:
                    copy(block, out_ref.at[pl.ds(pl.multiple_of((place * 4 + part) * shard, shard), shard), :])
                else:
                    copy(block, out_ref.at[part, pl.ds(pl.multiple_of(place * shard, shard), shard), :])
                if has_tail and k % 2 == 0 and t == 0:
                    copy(source.at[at, pl.ds(shard, TAIL_ROWS), :], tail[0].at[place])
    for made in copies:
        made.wait()


def assemble(me, arrays, shard, shards, by_rows):
    width = arrays[0].shape[2]
    has_tail = arrays[0].shape[1] > shard
    out = [shape_of((4 * shards * shard, width) if by_rows else (4, shards * shard, width), BF16)]
    if has_tail:
        out.append(shape_of((shards, TAIL_ROWS, width), BF16))
    anywhere = pl.BlockSpec(memory_space=pl.ANY)
    return pl.pallas_call(
        partial(assemble_kernel, shard, shards // 2, by_rows, has_tail),
        out_shape=out,
        grid_spec=pltpu.PrefetchScalarGridSpec(
            num_scalar_prefetch=1,
            grid=(1,),
            in_specs=[anywhere] * 4,
            out_specs=[full_spec(made.shape) for made in out],
            scratch_shapes=[pltpu.SemaphoreType.DMA((4 * shards + shards,))],
        ),
        name="assemble",
    )(me, *arrays)


def slots_of(me_ref, part, place_z, core, depth):
    apart = part ^ me_ref[0]
    first = (apart >> core) & 1
    second = (apart >> (1 - core)) & 1
    return (first * 2 + second) * depth + lax.rem(place_z + depth - me_ref[1], depth)


def weight_grad_kernel(shard, depth, kind, has_tail, me_ref, *refs):
    count = {"rows": 2, "columns": 2, "attend": 4}[kind]
    inputs = refs[:count]
    tail_ref = refs[count] if has_tail else None
    keep_ref, send_ref, left_ref, stage_ref, sems = refs[-5:]
    step = pl.program_id(0)
    c0 = me_ref[2]
    width = stage_ref.shape[2]
    pieces = width // shard

    def each(j, act):
        for k in range(pieces):
            if kind == "rows":
                place_z, core, part = j, k // 4, k % 4
            else:
                place_z, core, part = k // 2, k % 2, j
            slot = slots_of(me_ref, part, place_z, core, depth)

            def both(target):
                act(
                    pltpu.make_async_copy(
                        stage_ref.at[j, pl.ds(k * shard, shard), :], target.at[slot, pl.ds(0, shard), :], sems.at[j, k]
                    )
                )
                if has_tail:
                    act(
                        pltpu.make_async_copy(
                            tail_ref.at[j, k], target.at[slot, pl.ds(shard, TAIL_ROWS), :], sems.at[j, pieces + k]
                        )
                    )

            @pl.when(c0 == core)
            def _():
                both(keep_ref)

            @pl.when(c0 != core)
            def _():
                both(send_ref)

    def flip(source):
        left_ref[...] = source[...].T

    if kind == "rows":
        flip(inputs[0])
        right = inputs[1]
    elif kind == "columns":
        pl.when(step == 0)(lambda: flip(inputs[0]))
        right = inputs[1]
    else:
        pl.when(step == 0)(lambda: flip(inputs[0]))
        pl.when(step == 3)(lambda: flip(inputs[1]))
        right = None

    def multiply(right):
        rows = min(256, width)
        for at in range(0, width, rows):
            stage_ref[step, at : at + rows, :] = nn(left_ref[at : at + rows, :], right).astype(BF16)

    if kind == "attend":
        pl.when(step < 3)(lambda: multiply(inputs[2][0]))
        pl.when(step == 3)(lambda: multiply(inputs[3][...]))
    else:
        multiply(right[...])
    each(step, lambda made: made.start())

    @pl.when(step == pl.num_programs(0) - 1)
    def _():
        for j in range(4):
            each(j, lambda made: made.wait())


def weight_grad(me, kind, inputs, tail, shard, shards):
    rows, width = inputs[0].shape[0], min(inputs[0].shape[-1], inputs[-1].shape[-1])
    whole = full_spec((rows, width))
    block = pl.BlockSpec((rows, width), lambda j, _: (0, j))
    specs = {
        "rows": [block, whole],
        "columns": [whole, block],
        "attend": [whole, whole, pl.BlockSpec((1, rows, width), lambda j, _: (jnp.minimum(j, 2), 0, 0)), whole],
    }[kind]
    anywhere = pl.BlockSpec(memory_space=pl.ANY)
    has_tail = tail is not None
    pieces = width // shard
    height = shard + (TAIL_ROWS if has_tail else 0)
    return pl.pallas_call(
        partial(weight_grad_kernel, shard, shards // 2, kind, has_tail),
        out_shape=(shape_of((2 * shards, height, width), BF16),) * 2,
        grid_spec=pltpu.PrefetchScalarGridSpec(
            num_scalar_prefetch=1,
            grid=(4,),
            in_specs=specs + [full_spec(tail.shape)] * has_tail if has_tail else specs,
            out_specs=[anywhere] * 2,
            scratch_shapes=[
                pltpu.VMEM((width, rows), BF16),
                pltpu.VMEM((4, width, width), BF16),
                pltpu.SemaphoreType.DMA((4, 2 * pieces)),
            ],
        ),
        cost_estimate=cost(8 * rows * width * width, *inputs),
        name="weight_grad_" + kind,
    )(me, *inputs, *([tail] if has_tail else []))


def add(*parts):
    return sum(part.astype(F32) for part in parts).astype(BF16)


def halves(keep, got):
    middle = keep.shape[0] // 2
    return add(keep[:middle], got[:middle]), add(keep[middle:], got[middle:])


def sum_chain(kept, got, shards):
    total = [add(kept[s], got[s]) for s in range(kept.shape[0])]
    return total[0], [along(total[s], shards, s) for s in range(1, kept.shape[0])]


def place_kernel(shard, factor, kind, me_ref, in_ref, *outs):
    step = pl.program_id(0)
    value = in_ref[0, 0:shard, :].astype(F32) * factor
    if kind == "attend":
        pl.when(step < 3)(lambda: outs[0].__setitem__(..., value))
        pl.when(step == 3)(lambda: outs[1].__setitem__(..., value))
    else:
        outs[0][...] = value


def place_blocks(me, blocks, kind, shard, factor):
    _, height, width = blocks.shape

    def source(j, me_ref):
        apart = j ^ me_ref[0]
        first = (apart >> me_ref[2]) & 1
        second = (apart >> (1 - me_ref[2])) & 1
        return (first * 2 + second, 0, 0)

    out_shape, out_specs = {
        "rows": ([(4 * shard, width)], [pl.BlockSpec((shard, width), lambda j, _: (j, 0))]),
        "columns": ([(shard, 4 * width)], [pl.BlockSpec((shard, width), lambda j, _: (0, j))]),
        "attend": (
            [(shard, 3 * width), (shard, width)],
            [
                pl.BlockSpec((shard, width), lambda j, _: (0, jnp.minimum(j, 2))),
                pl.BlockSpec((shard, width), lambda j, _: (0, 0)),
            ],
        ),
    }[kind]
    return pl.pallas_call(
        partial(place_kernel, shard, factor, kind),
        out_shape=[shape_of(dims, F32) for dims in out_shape],
        grid_spec=pltpu.PrefetchScalarGridSpec(
            num_scalar_prefetch=1,
            grid=(4,),
            in_specs=[pl.BlockSpec((1, height, width), source)],
            out_specs=out_specs,
        ),
        name="place_" + kind,
    )(me, blocks)


def pack_rows(vectors, shards, width):
    packed = jnp.concatenate([v.reshape(shards, -1) for v in vectors], axis=1)
    packed = packed.reshape(shards, 4, -1).transpose(1, 0, 2).astype(BF16)
    return jnp.pad(packed[:, :, None, :], ((0, 0), (0, 0), (0, TAIL_ROWS - 1), (0, width - packed.shape[2])))


def unpack_rows(me, blocks, shard, sizes, factor):
    total = sum(sizes) * shard
    rows = blocks[:, shard, : total // 4].astype(F32) * factor
    ordered = []
    for j in range(4):
        apart = j ^ me[0]
        at = ((apart >> me[2]) & 1) * 2 + ((apart >> (1 - me[2])) & 1)
        ordered.append(lax.dynamic_index_in_dim(rows, at, 0, keepdims=False))
    flat = jnp.concatenate(ordered)
    out = []
    at = 0
    for size in sizes:
        out.append(flat[at * shard : (at + size) * shard])
        at += size
    return out


def vector_rows(*vectors):
    return jnp.stack([v.astype(F32) for v in vectors] + [jnp.zeros_like(vectors[0], F32)] * (8 - len(vectors)))


def split_small(small_full, shard, sizes):
    parts = []
    at = 0
    for size in sizes:
        parts.append(small_full[:, at * shard : (at + size) * shard].reshape(-1).astype(F32))
        at += size
    return parts


SMALL_ATTEND = (2, 1, 1, 1)
SMALL_FEED = (4, 1, 1, 1)


def per_device(
    tokens,
    segments,
    project_weight,
    project_bias,
    combine_weight,
    combine_bias,
    first_gain,
    first_shift,
    expand_weight,
    expand_bias,
    reduce_weight,
    reduce_bias,
    second_gain,
    second_shift,
    layer_cotangent,
    pooled_cotangent,
):
    row_count, length, width = tokens.shape
    shard = combine_weight.shape[0]
    shards = lax.axis_size("fsdp")
    flat = tokens.reshape(length, width)
    seg = segments.reshape(length)
    seg_row = segments
    seg_column = seg.reshape(length, 1)
    block = 256
    limits = key_limits(seg, block)
    replica, member = lax.axis_index("grp"), lax.axis_index("fsdp")
    me = jnp.stack([replica, member // 2, member % 2]).astype(jnp.int32)
    fast = lax.axis_size("grp") == 4 and shards % 2 == 0 and shard % 32 == 0 and width == shard * 8
    small = jnp.concatenate(
        [project_bias, combine_bias, first_gain, first_shift, expand_bias, reduce_bias, second_gain, second_shift]
    )

    if fast:
        lead = jnp.where(
            replica < 3,
            lax.dynamic_slice(project_weight, (0, jnp.minimum(replica, 2) * width), (shard, width)),
            combine_weight,
        )
        rows = jnp.pad(small, (0, TAIL_ROWS * width - small.shape[0])).reshape(TAIL_ROWS, width)
        lead = jnp.concatenate([lead, rows])
        chain_a = chain_of(lead, shards)
        part = after(lax.dynamic_slice(expand_weight, (0, replica * width), (shard, width)), chain_a)
        chain_e = chain_of(part, shards)
        near_a = near_of(chain_a, shards)
        far_a = swap_second(near_a, shards)
        arrays = (near_a, far_a, swap_core(near_a, shards), swap_core(far_a, shards))
        attend_full, small_full = assemble(me, arrays, shard, shards, False)
        small_full = small_full.reshape(shards, -1)
        near_e = near_of(after(chain_e, far_a), shards)
    else:
        attend_shard = jnp.concatenate(
            [project_weight.reshape(shard, 3, width).transpose(1, 0, 2), combine_weight[None]], axis=0
        )
        expand_shard = expand_weight.reshape(shard, 4, width).transpose(1, 0, 2)
        attend_full = lax.all_gather(attend_shard, "fsdp", axis=1, tiled=True)
        small_full = lax.all_gather(small, "fsdp", axis=0, tiled=False)
        expand_full = lax.all_gather(expand_shard, "fsdp", axis=1, tiled=True)
        reduce_full = lax.all_gather(reduce_weight, "fsdp", axis=0, tiled=True)
    bias_pair, bias_combine, gain_one, shift_one, bias_expand, bias_reduce, gain_two, shift_two = split_small(
        small_full, shard, SMALL_ATTEND + SMALL_FEED
    )
    bias_all = jnp.stack([bias_pair[:width], jnp.zeros((width,), F32), bias_pair[width:]]).reshape(3, 1, width)

    qkv = project(flat, attend_full, bias_all)
    if fast:
        qkv = after(qkv, near_e)
        far_e = swap_second(near_e, shards)
        part = lax.dynamic_slice(reduce_weight, (replica * shard, 0), (shard, width))
        chain_r = chain_of(after(part, near_e), shards)
    context, lse = attend_forward(qkv, limits, seg_column, seg_row, block)
    vec_one = vector_rows(bias_combine, gain_one, shift_one)
    vec_two = vector_rows(bias_reduce, gain_two, shift_two)
    if fast:
        context = after(context, far_e, chain_r)
        arrays = (near_e, far_e, swap_core(near_e, shards), swap_core(far_e, shards))
        near_r = near_of(chain_r, shards)
    hidden, hidden_low, normed, inverse = combine(context, attend_full, flat, vec_one, 256)
    if fast:
        hidden_low, *arrays = lax.optimization_barrier((hidden_low, *arrays, near_r))[:-1]
        expand_full = assemble(me, arrays, shard, shards, False)[0]
        far_r = swap_second(near_r, shards)
    act, slope = expand(hidden_low, expand_full, bias_expand.reshape(4, 1, width))
    if fast:
        act, far_r = lax.optimization_barrier((act, far_r))
        arrays = (near_r, far_r, swap_core(near_r, shards), swap_core(far_r, shards))
        reduce_full = assemble(me, arrays, shard, shards, True)[0]
    result_low, pooled, grad_second, grad_branch, sums_two = reduce(
        act,
        reduce_full,
        hidden,
        vec_two,
        layer_cotangent.reshape(length, width),
        pooled_cotangent.reshape(SEG, width),
        seg_column,
        seg_row,
        256,
    )
    factor = float(length * lax.axis_size("grp") * shards) ** (-0.5)
    if fast:
        keep_r, send_r = weight_grad(me, "rows", (act, grad_branch), None, shard, shards)
        got = swap_core(send_r, shards)
        grad_branch = after(grad_branch, send_r)
    grad_pre, sums_pre = grad_pre_of(grad_branch, reduce_full, slope)
    feed_vectors = [sums_pre[0], sums_two[2], sums_two[0], sums_two[1]]
    if fast:
        grad_pre, got = lax.optimization_barrier((grad_pre, got))
        keep_r, send_r = halves(keep_r, got)
        got_r = swap_first(send_r, shards)
        rows = pack_rows(feed_vectors, shards, width)
        keep_e, send_e = weight_grad(me, "columns", (hidden_low, after(grad_pre, send_r)), rows, shard, shards)
        send_e, got_r = lax.optimization_barrier((send_e, got_r))
        got_e = swap_core(send_e, shards)
        keep_r, send_r = halves(keep_r, got_r)
        got_r = swap_second(send_r, shards)
        grad_pre = after(grad_pre, send_e, send_r)
    grad_first, grad_attn, grad_context, sums_one = grad_hidden_of(
        grad_pre, expand_full, grad_second, normed, inverse, vec_one, attend_full, 256
    )
    if fast:
        pieces = 2
        grad_context, got_e, got_r = lax.optimization_barrier((grad_context, got_e, got_r))
        own_r, parts_r = sum_chain(keep_r, got_r, shards)
        keep_e, send_e = halves(keep_e, got_e)
        got_e = swap_first(send_e, shards)
        grad_qkv = attend_backward(
            qkv, after(grad_context, own_r, send_e), lse, limits, seg_column, seg_row, block, 0, pieces
        )
        first_qkv, got_e, *parts_r = lax.optimization_barrier((grad_qkv[0], got_e, *parts_r))
        own_r = add(own_r, *parts_r)
        pair_r = jnp.stack([own_r, swap_second(own_r, shards)])
        keep_e, send_e = halves(keep_e, got_e)
        got_e = swap_second(send_e, shards)
        grad_qkv = attend_backward(
            qkv,
            after(grad_context, send_e, own_r),
            lse,
            limits,
            seg_column,
            seg_row,
            block,
            pieces,
            pieces,
            (first_qkv, grad_qkv[1]),
        )
        first_qkv, got_e, pair_r = lax.optimization_barrier((grad_qkv[0], got_e, pair_r))
        reduce_blocks = jnp.concatenate([pair_r, swap_first(pair_r, shards)])
        own_e, parts_e = sum_chain(keep_e, got_e, shards)
        grad_qkv, sums_qkv = attend_backward(
            qkv,
            after(grad_context, own_e),
            lse,
            limits,
            seg_column,
            seg_row,
            block,
            2 * pieces,
            width // LANES - 2 * pieces,
            (first_qkv, grad_qkv[1]),
        )
        grad_qkv, *parts_e = lax.optimization_barrier((grad_qkv, *parts_e))
        own_e = add(own_e, *parts_e)
        pair_e = jnp.stack([own_e, swap_second(own_e, shards)])
    else:
        grad_qkv, sums_qkv = attend_backward(
            qkv, grad_context, lse, limits, seg_column, seg_row, block, 0, width // LANES
        )
    attend_vectors = [jnp.concatenate([sums_qkv[0], sums_qkv[2]]), sums_one[2], sums_one[0], sums_one[1]]
    if fast:
        rows = pack_rows(attend_vectors, shards, width)
        keep_a, send_a = weight_grad(
            me, "attend", (flat, context, after(grad_qkv, own_e), grad_attn), rows, shard, shards
        )
        send_a, pair_e = lax.optimization_barrier((send_a, pair_e))
        expand_blocks = jnp.concatenate([pair_e, swap_first(pair_e, shards)])
        got_a = swap_core(send_a, shards)
        keep_a, send_a = halves(keep_a, got_a)
        got_a = swap_first(send_a, shards)
        token_grad = token_grad_of(after(grad_qkv, send_a), attend_full, grad_first, 256)
        token_grad, got_a = lax.optimization_barrier((token_grad, got_a))
        keep_a, send_a = halves(keep_a, got_a)
        own_a, parts_a = sum_chain(keep_a, swap_second(send_a, shards), shards)
        own_a = add(own_a, *parts_a)
        pair_a = jnp.stack([own_a, swap_second(own_a, shards)])
        attend_blocks = jnp.concatenate([pair_a, swap_first(pair_a, shards)])
    else:
        token_grad = token_grad_of(grad_qkv, attend_full, grad_first, 256)

    if fast:
        reduce_grad = place_blocks(me, reduce_blocks, "rows", shard, factor)[0]
        expand_grad = place_blocks(me, expand_blocks, "columns", shard, factor)[0]
        project_grad, combine_grad = place_blocks(me, attend_blocks, "attend", shard, factor)
        small_grads = unpack_rows(me, attend_blocks, shard, SMALL_ATTEND, factor)
        small_grads += unpack_rows(me, expand_blocks, shard, SMALL_FEED, factor)
    else:

        def finish(term, axis):
            part = lax.psum_scatter(term.astype(BF16), "fsdp", scatter_dimension=axis, tiled=True)
            return lax.psum(part, "grp").astype(F32) * factor

        reduce_grad = finish(tn(act, grad_branch), 0)
        grad = jnp.stack([tn(hidden_low, grad_pre[:, t * width : (t + 1) * width]) for t in range(4)])
        expand_grad = finish(grad, 1).transpose(1, 0, 2).reshape(shard, 4 * width)
        grad = finish(jnp.stack([tn(flat, grad_qkv[t]) for t in range(3)] + [tn(context, grad_attn)]), 1)
        project_grad, combine_grad = grad[:3].transpose(1, 0, 2).reshape(shard, 3 * width), grad[3]
        packed = jnp.concatenate([v.reshape(shards, -1) for v in attend_vectors + feed_vectors], axis=1).reshape(-1)
        packed = lax.psum(lax.psum_scatter(packed, "fsdp", scatter_dimension=0, tiled=True), "grp") * factor
        small_grads = split_small(packed[None], shard, SMALL_ATTEND + SMALL_FEED)
    return (
        result_low.reshape(row_count, length, width),
        pooled.reshape(row_count, SEG, width),
        token_grad.reshape(row_count, length, width),
        project_grad,
        small_grads[0],
        combine_grad,
        small_grads[1],
        small_grads[2],
        small_grads[3],
        expand_grad,
        small_grads[4],
        reduce_grad,
        small_grads[5],
        small_grads[6],
        small_grads[7],
    )


def solution(mesh):
    in_specs = (
        P(("grp", "fsdp"), None, None),
        P(("grp", "fsdp"), None),
        P("fsdp", None),
        P("fsdp"),
        P("fsdp", None),
        P("fsdp"),
        P("fsdp"),
        P("fsdp"),
        P("fsdp", None),
        P("fsdp"),
        P("fsdp", None),
        P("fsdp"),
        P("fsdp"),
        P("fsdp"),
        P(("grp", "fsdp"), None, None),
        P(("grp", "fsdp"), None, None),
    )
    out_specs = (
        P(("grp", "fsdp"), None, None),
        P(("grp", "fsdp"), None, None),
        P(("grp", "fsdp"), None, None),
        P("fsdp", None),
        P("fsdp"),
        P("fsdp", None),
        P("fsdp"),
        P("fsdp"),
        P("fsdp"),
        P("fsdp", None),
        P("fsdp"),
        P("fsdp", None),
        P("fsdp"),
        P("fsdp"),
        P("fsdp"),
    )
    return jax.shard_map(
        per_device, mesh=mesh, in_specs=in_specs, out_specs=out_specs, check_vma=False
    )
```

```python
from functools import partial

import jax
import jax.numpy as jnp
from jax import lax
from jax.experimental import pallas as pl
from jax.experimental.pallas import tpu as pltpu
from jax.sharding import PartitionSpec as P

H = 12
DH = 64
SEG = 8
LANES = 128
NEG_FILL = -1e30
EPSILON = 1e-12
BF16 = jnp.bfloat16
F32 = jnp.float32

TAIL_P = 0.33
TAIL = (
    0.13275454438237264,
    0.11835055488372218,
    0.18469205342974412,
    -0.0957394408156175,
    0.3375615034491361,
    -0.2238704213061762,
    0.04625121306008233,
)
LOG2E = 1.4426950408889634
INV_SQRT_2PI = 0.3989422804014327


def cost(flops, *arrays):
    moved = sum(a.size * a.dtype.itemsize for a in arrays)
    return pl.CostEstimate(flops=int(flops), transcendentals=0, bytes_accessed=int(moved))


def nn(left, right):
    return lax.dot_general(left, right, (((1,), (0,)), ((), ())), preferred_element_type=F32)


def nt(left, right):
    return lax.dot_general(left, right, (((1,), (1,)), ((), ())), preferred_element_type=F32)


def tn(left, right):
    return lax.dot_general(left, right, (((0,), (0,)), ((), ())), preferred_element_type=F32)


def shape_of(dims, kind):
    return jax.ShapeDtypeStruct(dims, kind)


def full_spec(dims):
    return pl.BlockSpec(dims, lambda *_: (0,) * len(dims))


def normal_parts(x):
    bell = jnp.exp2(x * x * (-0.5 * LOG2E))
    t = 1.0 / (1.0 + TAIL_P * jnp.abs(x))
    poly = jnp.full_like(t, TAIL[-1])
    for coefficient in TAIL[-2::-1]:
        poly = poly * t + coefficient
    tail = poly * t * bell
    return jnp.where(x >= 0, 1.0 - tail, tail), bell * INV_SQRT_2PI


def project_kernel(x_ref, w_ref, b_ref, o_ref):
    rows = x_ref.shape[0]
    step = min(256, rows)
    for at in range(0, rows, step):
        o_ref[0, at : at + step, :] = (nn(x_ref[at : at + step, :], w_ref[0]) + b_ref[0]).astype(BF16)


def project(x, weights, bias):
    rows, width = x.shape
    half = width // 2
    return pl.pallas_call(
        project_kernel,
        out_shape=shape_of((3, rows, width), BF16),
        grid=(3, 2),
        in_specs=[
            full_spec((rows, width)),
            pl.BlockSpec((1, width, half), lambda t, j: (t, 0, j)),
            pl.BlockSpec((1, 1, half), lambda t, j: (t, 0, j)),
        ],
        out_specs=pl.BlockSpec((1, rows, half), lambda t, j: (t, 0, j)),
        cost_estimate=cost(6 * rows * width * width, x, weights),
        name="project",
    )(x, weights, bias)


MASKED = -1e30


def window_sizes(block, length):
    sizes = [block + extra for extra in (128, 256, 384, 512) if block + extra < length]
    return sizes + [length]


def key_limits(seg, block):
    length = seg.shape[0]
    rows = seg.reshape(length // block, block)
    place = jnp.arange(length, dtype=jnp.int32)[None, :]
    low = jnp.min(jnp.where(seg[None, :] == rows[:, :1], place, length), axis=1)
    high = jnp.max(jnp.where(seg[None, :] == rows[:, -1:], place + 1, 0), axis=1)
    low = low // LANES * LANES
    sizes = window_sizes(block, length)
    size = jnp.full_like(low, sizes[-1])
    for candidate in sizes[-2::-1]:
        size = jnp.where(high - low <= candidate, candidate, size)
    return jnp.stack([jnp.minimum(low, length - size), size])


def for_window(limits_ref, block, sizes, body):
    start = limits_ref[0, block]
    for size in sizes:

        @pl.when(limits_ref[1, block] == size)
        def _(size=size):
            body(pl.multiple_of(start, LANES), size)


def chunks_of(size, most):
    return [(at, min(most, size - at)) for at in range(0, size, most)]


def head_lanes():
    lane = lax.broadcasted_iota(jnp.int32, (1, LANES), 1)
    first = lane < DH
    return (first, jnp.logical_not(first)), lane % DH


def mask_keys(k_ref, seg_ref, kx_ref):
    mine, lane = head_lanes()
    keys = k_ref[0]
    outside = jnp.where(seg_ref[...] == lane, 0.0, jnp.where(lane <= SEG, MASKED, 0.0)).astype(BF16)
    for h in range(2):
        kx_ref[h] = jnp.where(mine[h], keys, outside)


def mask_queries(query, seg):
    mine, lane = head_lanes()
    inside = (seg == lane).astype(BF16)
    return [jnp.where(own, query, inside) for own in mine]


def attend_forward_kernel(
    sizes, limits_ref, q_ref, k_ref, v_ref, segq_ref, segk_ref, o_ref, lse_ref, kx_ref, vt_ref, s_ref
):
    block = pl.program_id(1)

    @pl.when(block == 0)
    def _():
        mask_keys(k_ref, segk_ref, kx_ref)
        vt_ref[...] = v_ref[0].T

    def body(start, size):
        queries = mask_queries(q_ref[0] * jnp.asarray(DH ** (-0.5), BF16), segq_ref[...])
        parts = []
        for h in range(2):
            highest = None
            for at, count in chunks_of(size, 128):
                scores = nt(kx_ref[h, pl.ds(start + at, count), :], queries[h])
                s_ref[h, at : at + count, :] = scores
                top = jnp.max(scores, axis=0, keepdims=True)
                highest = top if highest is None else jnp.maximum(highest, top)
            total = None
            out = None
            scaled = highest * LOG2E
            for at, count in chunks_of(size, 256):
                exponent = jnp.exp2(s_ref[h, at : at + count, :] * LOG2E - scaled)
                part = jnp.sum(exponent, axis=0, keepdims=True)
                total = part if total is None else total + part
                values = vt_ref[h * DH : (h + 1) * DH, pl.ds(start + at, count)]
                part = nn(values, exponent.astype(BF16))
                out = part if out is None else out + part
            parts.append(out / total)
            lse_ref[0, h : h + 1, :] = scaled + jnp.log2(total)
        o_ref[...] = jnp.concatenate(parts).T.astype(BF16)

    for_window(limits_ref, block, sizes, body)


def attend_forward(qkv, limits, seg_column, block):
    _, length, width = qkv.shape
    pairs = width // LANES
    return pl.pallas_call(
        partial(attend_forward_kernel, window_sizes(block, length)),
        out_shape=(shape_of((length, width), BF16), shape_of((pairs, 8, length), F32)),
        grid_spec=pltpu.PrefetchScalarGridSpec(
            num_scalar_prefetch=1,
            grid=(pairs, length // block),
            in_specs=[
                pl.BlockSpec((1, block, LANES), lambda p, b, _: (0, b, p)),
                pl.BlockSpec((1, length, LANES), lambda p, b, _: (1, 0, p)),
                pl.BlockSpec((1, length, LANES), lambda p, b, _: (2, 0, p)),
                pl.BlockSpec((block, 1), lambda p, b, _: (b, 0)),
                pl.BlockSpec((length, 1), lambda p, b, _: (0, 0)),
            ],
            out_specs=[
                pl.BlockSpec((block, LANES), lambda p, b, _: (b, p)),
                pl.BlockSpec((1, 8, block), lambda p, b, _: (p, 0, b)),
            ],
            scratch_shapes=[
                pltpu.VMEM((2, length, LANES), BF16),
                pltpu.VMEM((LANES, length), BF16),
                pltpu.VMEM((2, length, block), F32),
            ],
        ),
        cost_estimate=cost(8 * length * length * width, qkv),
        name="attend_forward",
    )(limits, qkv, qkv, qkv, seg_column, seg_column)


def attend_backward_kernel(
    sizes,
    limits_ref,
    q_ref,
    k_ref,
    v_ref,
    d_ref,
    o_ref,
    lse_ref,
    segq_ref,
    segk_ref,
    grad_ref,
    sums_ref,
    kx_ref,
    kt_ref,
    dk_ref,
    dv_ref,
    dq_ref,
):
    block = pl.program_id(1)
    rows = q_ref.shape[1]
    mine, _ = head_lanes()

    @pl.when(block == 0)
    def _():
        dk_ref[...] = jnp.zeros_like(dk_ref)
        dv_ref[...] = jnp.zeros_like(dv_ref)
        mask_keys(k_ref, segk_ref, kx_ref)
        kt_ref[...] = k_ref[0].T

    def body(start, size):
        query = q_ref[0] * jnp.asarray(DH ** (-0.5), BF16)
        grads = d_ref[...]
        none = jnp.zeros_like(query)
        queries = mask_queries(query, segq_ref[...])
        plain = jnp.concatenate([jnp.where(own, query, none) for own in mine])
        pulls = [jnp.where(own, grads, none) for own in mine]
        pulled = jnp.concatenate(pulls)
        products = (grads.astype(F32) * o_ref[...].astype(F32)).T
        inner = [jnp.sum(products[h * DH : (h + 1) * DH], axis=0, keepdims=True) for h in range(2)]
        grad_query = [None, None]
        for at, count in chunks_of(size, 256):
            place = pl.ds(start + at, count)
            values = v_ref[0, place, :]
            weights_low = []
            grads_low = []
            for h in range(2):
                scores = nt(kx_ref[h, place, :], queries[h])
                weights = jnp.exp2(scores * LOG2E - lse_ref[0, h : h + 1, :])
                grad_scores = (weights * (nt(values, pulls[h]) - inner[h])).astype(BF16)
                weights_low.append(weights.astype(BF16))
                grads_low.append(grad_scores)
                part = nn(kt_ref[h * DH : (h + 1) * DH, place], grad_scores)
                grad_query[h] = part if grad_query[h] is None else grad_query[h] + part
            dv_ref[place, :] += nn(jnp.concatenate(weights_low, axis=1), pulled)
            dk_ref[place, :] += nn(jnp.concatenate(grads_low, axis=1), plain)
        place = pl.ds(pl.multiple_of(block * rows, rows), rows)
        dq_ref[place, :] = jnp.concatenate(grad_query).T * (DH ** (-0.5))

    for_window(limits_ref, block, sizes, body)

    @pl.when(block == pl.num_programs(1) - 1)
    def _():
        for t, source in enumerate((dq_ref, dk_ref, dv_ref)):
            low = source[...].astype(BF16)
            grad_ref[t] = low
            if t != 1:
                sums_ref[t : t + 1, :] = jnp.sum(low.astype(F32), axis=0, keepdims=True)


def attend_backward(qkv, grad_context, context, lse, limits, seg_column, block, base, pairs, earlier=None):
    _, length, width = qkv.shape
    anywhere = pl.BlockSpec(memory_space=pl.ANY)
    made = (shape_of((3, length, width), BF16), shape_of((8, width), F32))
    kernel = partial(attend_backward_kernel, window_sizes(block, length))
    if earlier is not None:
        inner = kernel

        def kernel(limits_ref, *refs):
            inner(limits_ref, *refs[:8], *refs[10:])

    return pl.pallas_call(
        kernel,
        out_shape=made,
        grid_spec=pltpu.PrefetchScalarGridSpec(
            num_scalar_prefetch=1,
            grid=(pairs, length // block),
            in_specs=[
                pl.BlockSpec((1, block, LANES), lambda p, b, _: (0, b, base + p)),
                pl.BlockSpec((1, length, LANES), lambda p, b, _: (1, 0, base + p)),
                pl.BlockSpec((1, length, LANES), lambda p, b, _: (2, 0, base + p)),
                pl.BlockSpec((block, LANES), lambda p, b, _: (b, base + p)),
                pl.BlockSpec((block, LANES), lambda p, b, _: (b, base + p)),
                pl.BlockSpec((1, 8, block), lambda p, b, _: (base + p, 0, b)),
                pl.BlockSpec((block, 1), lambda p, b, _: (b, 0)),
                pl.BlockSpec((length, 1), lambda p, b, _: (0, 0)),
            ]
            + ([] if earlier is None else [anywhere] * 2),
            out_specs=[
                pl.BlockSpec((3, length, LANES), lambda p, b, _: (0, 0, base + p)),
                pl.BlockSpec((8, LANES), lambda p, b, _: (0, base + p)),
            ],
            scratch_shapes=[pltpu.VMEM((2, length, LANES), BF16), pltpu.VMEM((LANES, length), BF16)]
            + [pltpu.VMEM((length, LANES), F32)] * 3,
        ),
        input_output_aliases={} if earlier is None else {9: 0, 10: 1},
        cost_estimate=cost(12 * length * length * LANES * pairs, qkv),
        name="attend_backward",
    )(limits, qkv, qkv, qkv, grad_context, context, lse, seg_column, seg_column, *(earlier or ()))


def norm_values(values, gain, shift):
    average = jnp.mean(values, axis=-1, keepdims=True)
    centred = values - average
    variance = jnp.mean(centred * centred, axis=-1, keepdims=True)
    inverse = lax.rsqrt(variance + EPSILON)
    normed = centred * inverse
    return normed * gain + shift, normed, inverse


def norm_pull(grad_out, normed, inverse, gain):
    scaled = grad_out * gain
    mean_scaled = jnp.mean(scaled, axis=-1, keepdims=True)
    mean_product = jnp.mean(scaled * normed, axis=-1, keepdims=True)
    return inverse * (scaled - mean_scaled - normed * mean_product)


def column_sum(values):
    return jnp.sum(values, axis=0, keepdims=True)


def combine_kernel(c_ref, w_ref, x_ref, vec_ref, hidden_ref, low_ref, normed_ref, inverse_ref):
    attn = nn(c_ref[...], w_ref[0]) + vec_ref[0:1, :]
    hidden, normed, inverse = norm_values(x_ref[...].astype(F32) + attn, vec_ref[1:2, :], vec_ref[2:3, :])
    hidden_ref[...] = hidden
    low_ref[...] = hidden.astype(BF16)
    normed_ref[...] = normed
    inverse_ref[...] = inverse


def combine(context, weights, tokens, vectors, block):
    rows, width = context.shape
    row_spec = pl.BlockSpec((block, width), lambda b: (b, 0))
    return pl.pallas_call(
        combine_kernel,
        out_shape=(
            shape_of((rows, width), F32),
            shape_of((rows, width), BF16),
            shape_of((rows, width), F32),
            shape_of((rows, 1), F32),
        ),
        grid=(rows // block,),
        in_specs=[
            row_spec,
            pl.BlockSpec((1, width, width), lambda b: (3, 0, 0)),
            row_spec,
            full_spec(vectors.shape),
        ],
        out_specs=[row_spec, row_spec, row_spec, pl.BlockSpec((block, 1), lambda b: (b, 0))],
        cost_estimate=cost(4 * rows * width * width, context, tokens),
        name="combine",
    )(context, weights, tokens, vectors)


def expand_kernel(x_ref, w_ref, b_ref, act_ref, slope_ref):
    rows = x_ref.shape[0]
    step = min(256, rows)
    for at in range(0, rows, step):
        pre = nn(x_ref[at : at + step, :], w_ref[0]) + b_ref[0]
        mass, bell = normal_parts(pre)
        act_ref[at : at + step, :] = (pre * mass).astype(BF16)
        slope_ref[at : at + step, :] = (mass + pre * bell).astype(BF16)


def expand(hidden_low, weights, bias):
    rows, width = hidden_low.shape
    count = weights.shape[0]
    half = width // 2
    out_spec = pl.BlockSpec((rows, half), lambda t, j: (0, 2 * t + j))
    return pl.pallas_call(
        expand_kernel,
        out_shape=(shape_of((rows, count * width), BF16),) * 2,
        grid=(count, 2),
        in_specs=[
            full_spec((rows, width)),
            pl.BlockSpec((1, width, half), lambda t, j: (t, 0, j)),
            pl.BlockSpec((1, 1, half), lambda t, j: (t, 0, j)),
        ],
        out_specs=[out_spec, out_spec],
        cost_estimate=cost(12 * rows * count * width * width // 3, hidden_low, weights),
        name="expand",
    )(hidden_low, weights, bias)


def reduce_kernel(
    act_ref,
    w_ref,
    hidden_ref,
    vec_ref,
    cot_ref,
    pooled_cot_ref,
    seg_col_ref,
    seg_row_ref,
    out_ref,
    pooled_ref,
    grad_ref,
    grad_low_ref,
    sums_ref,
    share_ref,
):
    at = pl.program_id(0)
    rows = act_ref.shape[0]
    slot = lax.broadcasted_iota(jnp.int32, (16, 1), 0) + 1
    counts = jnp.sum((seg_row_ref[...] == slot).astype(F32), axis=1, keepdims=True)
    divisor = jnp.maximum(counts, 1.0)

    @pl.when(at == 0)
    def _():
        share_ref[...] = jnp.zeros_like(share_ref)
        share = pooled_cot_ref[...] / divisor[0:SEG]
        high = share.astype(BF16).astype(F32)
        share_ref[0:SEG, :] = high
        share_ref[2 * SEG : 3 * SEG, :] = share - high
        sums_ref[...] = jnp.zeros_like(sums_ref)
        pooled_ref[...] = jnp.zeros_like(pooled_ref)

    gain = vec_ref[1:2, :]
    branch = nn(act_ref[...], w_ref[...]) + vec_ref[0:1, :]
    result, normed, inverse = norm_values(hidden_ref[...] + branch, gain, vec_ref[2:3, :])
    out_ref[...] = result.astype(BF16)
    place = pl.ds(pl.multiple_of(at * rows, rows), rows)
    member = (seg_row_ref[:, place] == slot).astype(BF16)
    high = result.astype(BF16)
    rest = (result - high.astype(F32)).astype(BF16)
    pooled_ref[...] += (nn(member, high) + nn(member, rest))[0:SEG]
    lane = lax.broadcasted_iota(jnp.int32, (1, LANES), 1)
    chosen = jnp.where(lane < 2 * SEG, lane + 1, lane - 2 * SEG + 1)
    chosen = jnp.where(lane % (2 * SEG) < SEG, chosen, -1)
    chosen = jnp.where(lane < 4 * SEG, chosen, -1)
    spread = nn((seg_col_ref[...] == chosen).astype(BF16), share_ref[...].astype(BF16))
    grad_result = cot_ref[...].astype(F32) + spread
    grad_second = norm_pull(grad_result, normed, inverse, gain)
    grad_low = grad_second.astype(BF16)
    grad_ref[...] = grad_second
    grad_low_ref[...] = grad_low
    sums_ref[0:1, :] += column_sum(grad_result * normed)
    sums_ref[1:2, :] += column_sum(grad_result)
    sums_ref[2:3, :] += column_sum(grad_low.astype(F32))

    @pl.when(at == pl.num_programs(0) - 1)
    def _():
        pooled_ref[...] = pooled_ref[...] / divisor[0:SEG]


def reduce(act, weights, hidden, vectors, cotangent, pooled_cotangent, seg_column, seg_row, block):
    rows, width = hidden.shape
    depth = act.shape[1]
    row_spec = pl.BlockSpec((block, width), lambda b: (b, 0))
    return pl.pallas_call(
        reduce_kernel,
        out_shape=(
            shape_of((rows, width), BF16),
            shape_of((SEG, width), F32),
            shape_of((rows, width), F32),
            shape_of((rows, width), BF16),
            shape_of((8, width), F32),
        ),
        grid=(rows // block,),
        in_specs=[
            pl.BlockSpec((block, depth), lambda b: (b, 0)),
            full_spec(weights.shape),
            row_spec,
            full_spec(vectors.shape),
            row_spec,
            full_spec(pooled_cotangent.shape),
            pl.BlockSpec((block, 1), lambda b: (b, 0)),
            full_spec(seg_row.shape),
        ],
        out_specs=[
            row_spec,
            full_spec((SEG, width)),
            row_spec,
            row_spec,
            full_spec((8, width)),
        ],
        scratch_shapes=[pltpu.VMEM((LANES, width), F32)],
        cost_estimate=cost(3 * rows * width * depth, act, weights),
        name="reduce",
    )(act, weights, hidden, vectors, cotangent, pooled_cotangent, seg_column, seg_row)


def grad_pre_kernel(g_ref, w_ref, slope_ref, o_ref, sums_ref):
    rows = g_ref.shape[0]
    step = min(256, rows)
    total = None
    for at in range(0, rows, step):
        grad = nt(g_ref[at : at + step, :], w_ref[...]) * slope_ref[at : at + step, :].astype(F32)
        low = grad.astype(BF16)
        o_ref[at : at + step, :] = low
        part = column_sum(low.astype(F32))
        total = part if total is None else total + part
    sums_ref[...] = jnp.broadcast_to(total, sums_ref.shape)


def grad_pre_of(grad_branch, weights, slope):
    rows, width = grad_branch.shape
    depth = weights.shape[0]
    half = width // 2
    return pl.pallas_call(
        grad_pre_kernel,
        out_shape=(shape_of((rows, depth), BF16), shape_of((8, depth), F32)),
        grid=(depth // half,),
        in_specs=[
            full_spec((rows, width)),
            pl.BlockSpec((half, width), lambda j: (j, 0)),
            pl.BlockSpec((rows, half), lambda j: (0, j)),
        ],
        out_specs=[
            pl.BlockSpec((rows, half), lambda j: (0, j)),
            pl.BlockSpec((8, half), lambda j: (0, j)),
        ],
        cost_estimate=cost(3 * rows * width * depth, grad_branch, weights),
        name="grad_pre",
    )(grad_branch, weights, slope)


def grad_hidden_kernel(
    gp_ref, we_ref, second_ref, normed_ref, inverse_ref, vec_ref, wc_ref, first_ref, low_ref, context_ref, sums_ref
):
    @pl.when(pl.program_id(0) == 0)
    def _():
        sums_ref[...] = jnp.zeros_like(sums_ref)

    width = second_ref.shape[1]
    grad_hidden = second_ref[...]
    for t in range(we_ref.shape[0]):
        grad_hidden += nt(gp_ref[:, t * width : (t + 1) * width], we_ref[t])
    normed = normed_ref[...]
    grad_first = norm_pull(grad_hidden, normed, inverse_ref[...], vec_ref[1:2, :])
    low = grad_first.astype(BF16)
    first_ref[...] = grad_first
    low_ref[...] = low
    context_ref[...] = nt(low, wc_ref[0]).astype(BF16)
    sums_ref[0:1, :] += column_sum(grad_hidden * normed)
    sums_ref[1:2, :] += column_sum(grad_hidden)
    sums_ref[2:3, :] += column_sum(low.astype(F32))


def grad_hidden_of(grad_pre, expand_weights, grad_second, normed, inverse, vectors, attend_weights, block):
    rows, width = grad_second.shape
    row_spec = pl.BlockSpec((block, width), lambda b: (b, 0))
    return pl.pallas_call(
        grad_hidden_kernel,
        out_shape=(
            shape_of((rows, width), F32),
            shape_of((rows, width), BF16),
            shape_of((rows, width), BF16),
            shape_of((8, width), F32),
        ),
        grid=(rows // block,),
        in_specs=[
            pl.BlockSpec((block, grad_pre.shape[1]), lambda b: (b, 0)),
            full_spec(expand_weights.shape),
            row_spec,
            row_spec,
            pl.BlockSpec((block, 1), lambda b: (b, 0)),
            full_spec(vectors.shape),
            pl.BlockSpec((1, width, width), lambda b: (3, 0, 0)),
        ],
        out_specs=[row_spec, row_spec, row_spec, full_spec((8, width))],
        cost_estimate=cost(12 * rows * width * width, grad_pre, expand_weights),
        name="grad_hidden",
    )(grad_pre, expand_weights, grad_second, normed, inverse, vectors, attend_weights)


def token_grad_kernel(g_ref, w_ref, first_ref, o_ref):
    total = first_ref[...]
    for t in range(3):
        total += nt(g_ref[t], w_ref[t])
    o_ref[...] = total.astype(BF16)


def token_grad_of(grad_qkv, weights, grad_first, block):
    rows, width = grad_first.shape
    row_spec = pl.BlockSpec((block, width), lambda b: (b, 0))
    return pl.pallas_call(
        token_grad_kernel,
        out_shape=shape_of((rows, width), BF16),
        grid=(rows // block,),
        in_specs=[
            pl.BlockSpec((3, block, width), lambda b: (0, b, 0)),
            pl.BlockSpec((3, width, width), lambda b: (0, 0, 0)),
            row_spec,
        ],
        out_specs=row_spec,
        cost_estimate=cost(6 * rows * width * width, grad_qkv, weights),
        name="token_grad",
    )(grad_qkv, weights, grad_first)


AXES = ("grp", "fsdp")
TAIL_ROWS = 8


def hop(value, shards, move):
    pairs = []
    for g in range(4):
        for f in range(shards):
            to_g, to_f = move(g, f)
            pairs.append((g * shards + f, to_g * shards + to_f))
    return lax.ppermute(value, AXES, pairs)


def along(value, shards, by):
    return hop(value, shards, lambda g, f: (g, (f + 2 * by) % shards))


def swap_first(value, shards):
    return hop(value, shards, lambda g, f: (g ^ (1 + f % 2), f))


def swap_second(value, shards):
    return hop(value, shards, lambda g, f: (g ^ (2 - f % 2), f))


def swap_core(value, shards):
    return hop(value, shards, lambda g, f: (g, f ^ 1))


def after(value, *others):
    return lax.optimization_barrier((value, *others))[0]


def chain_of(block, shards):
    return jnp.stack([block] + [along(block, shards, by) for by in range(1, shards // 2)])


def near_of(chain, shards):
    return jnp.concatenate([chain, swap_first(chain, shards)])


def lead_kernel(shard, me_ref, p_ref, c_ref, *refs):
    vectors, out_ref = refs[:-1], refs[-1]
    pl.when(me_ref[0] < 3)(lambda: out_ref.__setitem__((slice(0, shard), slice(None)), p_ref[...]))
    pl.when(me_ref[0] == 3)(lambda: out_ref.__setitem__((slice(0, shard), slice(None)), c_ref[...]))
    rows = [
        jnp.pad(vector[...].astype(F32), ((0, 0), (0, out_ref.shape[1] - vector.shape[1]))) for vector in vectors
    ]
    out_ref[shard:, :] = jnp.concatenate(rows).astype(BF16)


def lead_block(me, project_weight, combine_weight, vectors):
    shard, width = combine_weight.shape
    vectors = [v[None] for v in vectors]
    return pl.pallas_call(
        partial(lead_kernel, shard),
        out_shape=shape_of((shard + TAIL_ROWS, width), BF16),
        grid_spec=pltpu.PrefetchScalarGridSpec(
            num_scalar_prefetch=1,
            grid=(1,),
            in_specs=[
                pl.BlockSpec((shard, width), lambda i, me_ref: (0, jnp.minimum(me_ref[0], 2))),
                full_spec(combine_weight.shape),
            ]
            + [full_spec(v.shape) for v in vectors],
            out_specs=full_spec((shard + TAIL_ROWS, width)),
        ),
        name="lead",
    )(me, project_weight, combine_weight, *vectors)


def assemble_kernel(shard, depth, by_rows, has_tail, me_ref, *refs):
    sources, (out_ref, *tail), sems = refs[:4], refs[4:-1], refs[-1]
    g0, z0, c0 = me_ref[0], me_ref[1], me_ref[2]
    copies = []

    def copy(source, target):
        made = pltpu.make_async_copy(source, target, sems.at[len(copies)])
        made.start()
        copies.append(made)

    for k, source in enumerate(sources):
        core = c0 if k < 2 else 1 - c0
        for t in range(2):
            part = g0 ^ (t * (1 + core)) ^ ((k % 2) * (2 - core))
            for s in range(depth):
                place = lax.rem(z0 + depth - s, depth) * 2 + core
                at = t * depth + s
                block = source.at[at, pl.ds(0, shard), :]
                if by_rows:
                    copy(block, out_ref.at[pl.ds(pl.multiple_of((place * 4 + part) * shard, shard), shard), :])
                else:
                    copy(block, out_ref.at[part, pl.ds(pl.multiple_of(place * shard, shard), shard), :])
                if has_tail and k % 2 == 0 and t == 0:
                    copy(source.at[at, pl.ds(shard, TAIL_ROWS), :], tail[0].at[place])
    for made in copies:
        made.wait()


def assemble(me, arrays, shard, shards, by_rows):
    width = arrays[0].shape[2]
    has_tail = arrays[0].shape[1] > shard
    out = [shape_of((4 * shards * shard, width) if by_rows else (4, shards * shard, width), BF16)]
    if has_tail:
        out.append(shape_of((shards, TAIL_ROWS, width), BF16))
    anywhere = pl.BlockSpec(memory_space=pl.ANY)
    return pl.pallas_call(
        partial(assemble_kernel, shard, shards // 2, by_rows, has_tail),
        out_shape=out,
        grid_spec=pltpu.PrefetchScalarGridSpec(
            num_scalar_prefetch=1,
            grid=(1,),
            in_specs=[anywhere] * 4,
            out_specs=[full_spec(made.shape) for made in out],
            scratch_shapes=[pltpu.SemaphoreType.DMA((4 * shards + shards,))],
        ),
        name="assemble",
    )(me, *arrays)


def slots_of(me_ref, part, place_z, core, depth):
    apart = part ^ me_ref[0]
    first = (apart >> core) & 1
    second = (apart >> (1 - core)) & 1
    return (first * 2 + second) * depth + lax.rem(place_z + depth - me_ref[1], depth)


def weight_grad_kernel(shard, depth, kind, has_tail, me_ref, *refs):
    count = {"rows": 2, "columns": 2, "attend": 4}[kind]
    inputs = refs[:count]
    tail_ref = refs[count] if has_tail else None
    keep_ref, send_ref, left_ref, stage_ref, sems = refs[-5:]
    step = pl.program_id(0)
    c0 = me_ref[2]
    width = stage_ref.shape[2]
    pieces = width // shard

    def each(j, act):
        for k in range(pieces):
            if kind == "rows":
                place_z, core, part = j, k // 4, k % 4
            else:
                place_z, core, part = k // 2, k % 2, j
            slot = slots_of(me_ref, part, place_z, core, depth)

            def both(target):
                act(
                    pltpu.make_async_copy(
                        stage_ref.at[j, pl.ds(k * shard, shard), :], target.at[slot, pl.ds(0, shard), :], sems.at[j, k]
                    )
                )
                if has_tail:
                    act(
                        pltpu.make_async_copy(
                            tail_ref.at[j, k], target.at[slot, pl.ds(shard, TAIL_ROWS), :], sems.at[j, pieces + k]
                        )
                    )

            @pl.when(c0 == core)
            def _():
                both(keep_ref)

            @pl.when(c0 != core)
            def _():
                both(send_ref)

    def flip(source):
        left_ref[...] = source[...].T

    if kind == "rows":
        flip(inputs[0])
        right = inputs[1]
    elif kind == "columns":
        pl.when(step == 0)(lambda: flip(inputs[0]))
        right = inputs[1]
    else:
        pl.when(step == 0)(lambda: flip(inputs[0]))
        pl.when(step == 3)(lambda: flip(inputs[1]))
        right = None

    def multiply(right):
        rows = min(256, width)
        for at in range(0, width, rows):
            stage_ref[step, at : at + rows, :] = nn(left_ref[at : at + rows, :], right).astype(BF16)

    if kind == "attend":
        pl.when(step < 3)(lambda: multiply(inputs[2][0]))
        pl.when(step == 3)(lambda: multiply(inputs[3][...]))
    else:
        multiply(right[...])
    each(step, lambda made: made.start())

    @pl.when(step == pl.num_programs(0) - 1)
    def _():
        for j in range(4):
            each(j, lambda made: made.wait())


def weight_grad(me, kind, inputs, tail, shard, shards):
    rows, width = inputs[0].shape[0], min(inputs[0].shape[-1], inputs[-1].shape[-1])
    whole = full_spec((rows, width))
    block = pl.BlockSpec((rows, width), lambda j, _: (0, j))
    specs = {
        "rows": [block, whole],
        "columns": [whole, block],
        "attend": [whole, whole, pl.BlockSpec((1, rows, width), lambda j, _: (jnp.minimum(j, 2), 0, 0)), whole],
    }[kind]
    anywhere = pl.BlockSpec(memory_space=pl.ANY)
    has_tail = tail is not None
    pieces = width // shard
    height = shard + (TAIL_ROWS if has_tail else 0)
    return pl.pallas_call(
        partial(weight_grad_kernel, shard, shards // 2, kind, has_tail),
        out_shape=(shape_of((2 * shards, height, width), BF16),) * 2,
        grid_spec=pltpu.PrefetchScalarGridSpec(
            num_scalar_prefetch=1,
            grid=(4,),
            in_specs=specs + [full_spec(tail.shape)] * has_tail if has_tail else specs,
            out_specs=[anywhere] * 2,
            scratch_shapes=[
                pltpu.VMEM((width, rows), BF16),
                pltpu.VMEM((4, width, width), BF16),
                pltpu.SemaphoreType.DMA((4, 2 * pieces)),
            ],
        ),
        cost_estimate=cost(8 * rows * width * width, *inputs),
        name="weight_grad_" + kind,
    )(me, *inputs, *([tail] if has_tail else []))


def add(*parts):
    return sum(part.astype(F32) for part in parts).astype(BF16)


def halves(keep, got):
    middle = keep.shape[0] // 2
    return add(keep[:middle], got[:middle]), add(keep[middle:], got[middle:])


def sum_chain(kept, got, shards):
    total = [add(kept[s], got[s]) for s in range(kept.shape[0])]
    return total[0], [along(total[s], shards, s) for s in range(1, kept.shape[0])]


def place_kernel(shard, factor, kind, me_ref, in_ref, *outs):
    step = pl.program_id(0)
    value = in_ref[0, 0:shard, :].astype(F32) * factor
    if kind == "attend":
        pl.when(step < 3)(lambda: outs[0].__setitem__(..., value))
        pl.when(step == 3)(lambda: outs[1].__setitem__(..., value))
    else:
        outs[0][...] = value


def place_blocks(me, blocks, kind, shard, factor):
    _, height, width = blocks.shape

    def source(j, me_ref):
        apart = j ^ me_ref[0]
        first = (apart >> me_ref[2]) & 1
        second = (apart >> (1 - me_ref[2])) & 1
        return (first * 2 + second, 0, 0)

    out_shape, out_specs = {
        "rows": ([(4 * shard, width)], [pl.BlockSpec((shard, width), lambda j, _: (j, 0))]),
        "columns": ([(shard, 4 * width)], [pl.BlockSpec((shard, width), lambda j, _: (0, j))]),
        "attend": (
            [(shard, 3 * width), (shard, width)],
            [
                pl.BlockSpec((shard, width), lambda j, _: (0, jnp.minimum(j, 2))),
                pl.BlockSpec((shard, width), lambda j, _: (0, 0)),
            ],
        ),
    }[kind]
    return pl.pallas_call(
        partial(place_kernel, shard, factor, kind),
        out_shape=[shape_of(dims, F32) for dims in out_shape],
        grid_spec=pltpu.PrefetchScalarGridSpec(
            num_scalar_prefetch=1,
            grid=(4,),
            in_specs=[pl.BlockSpec((1, height, width), source)],
            out_specs=out_specs,
        ),
        name="place_" + kind,
    )(me, blocks)


def pack_rows(vectors, shards, width):
    packed = jnp.concatenate([v.reshape(shards, -1) for v in vectors], axis=1)
    packed = packed.reshape(shards, 4, -1).transpose(1, 0, 2).astype(BF16)
    return jnp.pad(packed[:, :, None, :], ((0, 0), (0, 0), (0, TAIL_ROWS - 1), (0, width - packed.shape[2])))


def unpack_rows(me, blocks, shard, sizes, factor):
    total = sum(sizes) * shard
    rows = blocks[:, shard, : total // 4].astype(F32) * factor
    ordered = []
    for j in range(4):
        apart = j ^ me[0]
        at = ((apart >> me[2]) & 1) * 2 + ((apart >> (1 - me[2])) & 1)
        ordered.append(lax.dynamic_index_in_dim(rows, at, 0, keepdims=False))
    flat = jnp.concatenate(ordered)
    out = []
    at = 0
    for size in sizes:
        out.append(flat[at * shard : (at + size) * shard])
        at += size
    return out


def vector_rows(*vectors):
    return jnp.stack([v.astype(F32) for v in vectors] + [jnp.zeros_like(vectors[0], F32)] * (8 - len(vectors)))


def split_small(small_full, shard, sizes):
    parts = []
    at = 0
    for size in sizes:
        parts.append(small_full[:, at * shard : (at + size) * shard].reshape(-1).astype(F32))
        at += size
    return parts


SMALL_ATTEND = (2, 1, 1, 1)
SMALL_FEED = (4, 1, 1, 1)


def per_device(
    tokens,
    segments,
    project_weight,
    project_bias,
    combine_weight,
    combine_bias,
    first_gain,
    first_shift,
    expand_weight,
    expand_bias,
    reduce_weight,
    reduce_bias,
    second_gain,
    second_shift,
    layer_cotangent,
    pooled_cotangent,
):
    row_count, length, width = tokens.shape
    shard = combine_weight.shape[0]
    shards = lax.axis_size("fsdp")
    flat = tokens.reshape(length, width)
    seg = segments.reshape(length)
    seg_row = segments
    seg_column = seg.reshape(length, 1)
    block = 256
    limits = key_limits(seg, block)
    replica, member = lax.axis_index("grp"), lax.axis_index("fsdp")
    me = jnp.stack([replica, member // 2, member % 2]).astype(jnp.int32)
    fast = lax.axis_size("grp") == 4 and shards % 2 == 0 and shard % 32 == 0 and width == shard * 8
    small = [project_bias, combine_bias, first_gain, first_shift, expand_bias, reduce_bias, second_gain, second_shift]

    if fast:
        lead = lead_block(me, project_weight, combine_weight, small)
        chain_a = chain_of(lead, shards)
        part_e = lax.dynamic_slice(expand_weight, (0, replica * width), (shard, width))
        near_a = near_of(chain_a, shards)
        chain_e = chain_of(after(part_e, near_a), shards)
        far_a, chain_e = lax.optimization_barrier((swap_second(near_a, shards), chain_e))
        arrays = (near_a, far_a, swap_core(near_a, shards), swap_core(far_a, shards))
        attend_full, small_full = assemble(me, arrays, shard, shards, False)
        got_e = swap_first(after(chain_e, arrays[3]), shards)
        small_full = [small_full[:, k, : v.shape[0]].reshape(-1).astype(F32) for k, v in enumerate(small)]
    else:
        attend_shard = jnp.concatenate(
            [project_weight.reshape(shard, 3, width).transpose(1, 0, 2), combine_weight[None]], axis=0
        )
        expand_shard = expand_weight.reshape(shard, 4, width).transpose(1, 0, 2)
        attend_full = lax.all_gather(attend_shard, "fsdp", axis=1, tiled=True)
        small_full = split_small(
            lax.all_gather(jnp.concatenate(small), "fsdp", axis=0, tiled=False), shard, SMALL_ATTEND + SMALL_FEED
        )
        expand_full = lax.all_gather(expand_shard, "fsdp", axis=1, tiled=True)
        reduce_full = lax.all_gather(reduce_weight, "fsdp", axis=0, tiled=True)
    bias_pair, bias_combine, gain_one, shift_one, bias_expand, bias_reduce, gain_two, shift_two = small_full
    bias_all = jnp.stack([bias_pair[:width], jnp.zeros((width,), F32), bias_pair[width:]]).reshape(3, 1, width)

    qkv = project(flat, attend_full, bias_all)
    if fast:
        qkv, got_e = lax.optimization_barrier((qkv, got_e))
        near_e = jnp.concatenate([chain_e, got_e])
        far_e = swap_second(near_e, shards)
        part_r = lax.dynamic_slice(reduce_weight, (replica * shard, 0), (shard, width))
        chain_r = chain_of(after(part_r, qkv), shards)
    context, lse = attend_forward(qkv, limits, seg_column, block)
    vec_one = vector_rows(bias_combine, gain_one, shift_one)
    vec_two = vector_rows(bias_reduce, gain_two, shift_two)
    if fast:
        context, far_e, chain_r = lax.optimization_barrier((context, far_e, chain_r))
        arrays = (near_e, far_e, swap_core(near_e, shards), swap_core(far_e, shards))
        near_r = near_of(chain_r, shards)
    hidden, hidden_low, normed, inverse = combine(context, attend_full, flat, vec_one, 256)
    if fast:
        hidden_low, near_r, *arrays = lax.optimization_barrier((hidden_low, near_r, *arrays))
        expand_full = assemble(me, arrays, shard, shards, False)[0]
        far_r = swap_second(near_r, shards)
    act, slope = expand(hidden_low, expand_full, bias_expand.reshape(4, 1, width))
    if fast:
        act, far_r = lax.optimization_barrier((act, far_r))
        arrays = (near_r, far_r, swap_core(near_r, shards), swap_core(far_r, shards))
        reduce_full = assemble(me, arrays, shard, shards, True)[0]
    result_low, pooled, grad_second, grad_branch, sums_two = reduce(
        act,
        reduce_full,
        hidden,
        vec_two,
        layer_cotangent.reshape(length, width),
        pooled_cotangent.reshape(SEG, width),
        seg_column,
        seg_row,
        256,
    )
    factor = float(length * lax.axis_size("grp") * shards) ** (-0.5)
    if fast:
        keep_r, send_r = weight_grad(me, "rows", (act, grad_branch), None, shard, shards)
        got = swap_core(send_r, shards)
        grad_branch = after(grad_branch, send_r)
    grad_pre, sums_pre = grad_pre_of(grad_branch, reduce_full, slope)
    feed_vectors = [sums_pre[0], sums_two[2], sums_two[0], sums_two[1]]
    if fast:
        grad_pre, got = lax.optimization_barrier((grad_pre, got))
        keep_r, send_r = halves(keep_r, got)
        got_r = swap_first(send_r, shards)
        rows = pack_rows(feed_vectors, shards, width)
        keep_e, send_e = weight_grad(me, "columns", (hidden_low, after(grad_pre, send_r)), rows, shard, shards)
        send_e, got_r = lax.optimization_barrier((send_e, got_r))
        got_e = swap_core(send_e, shards)
        keep_r, send_r = halves(keep_r, got_r)
        got_r = swap_second(send_r, shards)
        grad_pre = after(grad_pre, send_e, send_r)
    grad_first, grad_attn, grad_context, sums_one = grad_hidden_of(
        grad_pre, expand_full, grad_second, normed, inverse, vec_one, attend_full, 256
    )
    if fast:
        pieces = 2
        grad_context, got_e, got_r = lax.optimization_barrier((grad_context, got_e, got_r))
        own_r, parts_r = sum_chain(keep_r, got_r, shards)
        keep_e, send_e = halves(keep_e, got_e)
        got_e = swap_first(send_e, shards)
        grad_qkv = attend_backward(
            qkv, after(grad_context, own_r, send_e), context, lse, limits, seg_column, block, 0, pieces
        )
        first_qkv, got_e, *parts_r = lax.optimization_barrier((grad_qkv[0], got_e, *parts_r))
        own_r = add(own_r, *parts_r)
        pair_r = jnp.stack([own_r, swap_second(own_r, shards)])
        keep_e, send_e = halves(keep_e, got_e)
        got_e = swap_second(send_e, shards)
        grad_qkv = attend_backward(
            qkv,
            after(grad_context, send_e, own_r),
            context,
            lse,
            limits,
            seg_column,
            block,
            pieces,
            pieces,
            (first_qkv, grad_qkv[1]),
        )
        first_qkv, got_e, pair_r = lax.optimization_barrier((grad_qkv[0], got_e, pair_r))
        reduce_blocks = jnp.concatenate([pair_r, swap_first(pair_r, shards)])
        own_e, parts_e = sum_chain(keep_e, got_e, shards)
        grad_qkv, sums_qkv = attend_backward(
            qkv,
            after(grad_context, own_e),
            context,
            lse,
            limits,
            seg_column,
            block,
            2 * pieces,
            width // LANES - 2 * pieces,
            (first_qkv, grad_qkv[1]),
        )
        grad_qkv, *parts_e = lax.optimization_barrier((grad_qkv, *parts_e))
        own_e = add(own_e, *parts_e)
        pair_e = jnp.stack([own_e, swap_second(own_e, shards)])
    else:
        grad_qkv, sums_qkv = attend_backward(
            qkv, grad_context, context, lse, limits, seg_column, block, 0, width // LANES
        )
    attend_vectors = [jnp.concatenate([sums_qkv[0], sums_qkv[2]]), sums_one[2], sums_one[0], sums_one[1]]
    if fast:
        rows = pack_rows(attend_vectors, shards, width)
        keep_a, send_a = weight_grad(
            me, "attend", (flat, context, after(grad_qkv, own_e), grad_attn), rows, shard, shards
        )
        send_a, pair_e = lax.optimization_barrier((send_a, pair_e))
        expand_blocks = jnp.concatenate([pair_e, swap_first(pair_e, shards)])
        got_a = swap_core(send_a, shards)
        keep_a, send_a = halves(keep_a, got_a)
        got_a = swap_first(send_a, shards)
        token_grad = token_grad_of(after(grad_qkv, send_a), attend_full, grad_first, 256)
        token_grad, got_a = lax.optimization_barrier((token_grad, got_a))
        keep_a, send_a = halves(keep_a, got_a)
        own_a, parts_a = sum_chain(keep_a, swap_second(send_a, shards), shards)
        own_a = add(own_a, *parts_a)
        pair_a = jnp.stack([own_a, swap_second(own_a, shards)])
        attend_blocks = jnp.concatenate([pair_a, swap_first(pair_a, shards)])
    else:
        token_grad = token_grad_of(grad_qkv, attend_full, grad_first, 256)

    if fast:
        reduce_grad = place_blocks(me, reduce_blocks, "rows", shard, factor)[0]
        expand_grad = place_blocks(me, expand_blocks, "columns", shard, factor)[0]
        project_grad, combine_grad = place_blocks(me, attend_blocks, "attend", shard, factor)
        small_grads = unpack_rows(me, attend_blocks, shard, SMALL_ATTEND, factor)
        small_grads += unpack_rows(me, expand_blocks, shard, SMALL_FEED, factor)
    else:

        def finish(term, axis):
            part = lax.psum_scatter(term.astype(BF16), "fsdp", scatter_dimension=axis, tiled=True)
            return lax.psum(part, "grp").astype(F32) * factor

        reduce_grad = finish(tn(act, grad_branch), 0)
        grad = jnp.stack([tn(hidden_low, grad_pre[:, t * width : (t + 1) * width]) for t in range(4)])
        expand_grad = finish(grad, 1).transpose(1, 0, 2).reshape(shard, 4 * width)
        grad = finish(jnp.stack([tn(flat, grad_qkv[t]) for t in range(3)] + [tn(context, grad_attn)]), 1)
        project_grad, combine_grad = grad[:3].transpose(1, 0, 2).reshape(shard, 3 * width), grad[3]
        packed = jnp.concatenate([v.reshape(shards, -1) for v in attend_vectors + feed_vectors], axis=1).reshape(-1)
        packed = lax.psum(lax.psum_scatter(packed, "fsdp", scatter_dimension=0, tiled=True), "grp") * factor
        small_grads = split_small(packed[None], shard, SMALL_ATTEND + SMALL_FEED)
    return (
        result_low.reshape(row_count, length, width),
        pooled.reshape(row_count, SEG, width),
        token_grad.reshape(row_count, length, width),
        project_grad,
        small_grads[0],
        combine_grad,
        small_grads[1],
        small_grads[2],
        small_grads[3],
        expand_grad,
        small_grads[4],
        reduce_grad,
        small_grads[5],
        small_grads[6],
        small_grads[7],
    )


def solution(mesh):
    in_specs = (
        P(("grp", "fsdp"), None, None),
        P(("grp", "fsdp"), None),
        P("fsdp", None),
        P("fsdp"),
        P("fsdp", None),
        P("fsdp"),
        P("fsdp"),
        P("fsdp"),
        P("fsdp", None),
        P("fsdp"),
        P("fsdp", None),
        P("fsdp"),
        P("fsdp"),
        P("fsdp"),
        P(("grp", "fsdp"), None, None),
        P(("grp", "fsdp"), None, None),
    )
    out_specs = (
        P(("grp", "fsdp"), None, None),
        P(("grp", "fsdp"), None, None),
        P(("grp", "fsdp"), None, None),
        P("fsdp", None),
        P("fsdp"),
        P("fsdp", None),
        P("fsdp"),
        P("fsdp"),
        P("fsdp"),
        P("fsdp", None),
        P("fsdp"),
        P("fsdp", None),
        P("fsdp"),
        P("fsdp"),
        P("fsdp"),
    )
    return jax.shard_map(
        per_device, mesh=mesh, in_specs=in_specs, out_specs=out_specs, check_vma=False
    )
```
